512 devices in a mesh: box: 64 (over y, z), row: 8 (over x, core).
Axes of the slice: x: 4, y: 4, z: 16, core: 2. Of those that a mesh axis runs over, the one named last changes fastest.
Arguments:
- rhs: float32 [512, 64, 320], P('box'), may hold values from -6 to 6
- skel1: int32 [512, 192], P('box'), may hold values from 0 to 319, as said below
- red1: int32 [512, 128], P('box'), may hold values from 0 to 319, as said below
- interp1: bfloat16 [512, 128, 192], P('box', None, 'row'), may hold values from -0.5 to 0.5
- inv1: bfloat16 [512, 128, 128], P('box', None, 'row'), may hold values from -0.5 to 0.5
- couple1: bfloat16 [512, 8, 128, 192], P('box', None, None, 'row'), may hold values from -0.5 to 0.5
- near1: int32 [512, 8], P('box'), may hold values from -1 to 511, as said below
- skel2: int32 [64, 384], P('box'), may hold values from 0 to 1535, as said below
- red2: int32 [64, 1152], P('box'), may hold values from 0 to 1535, as said below
- interp2: bfloat16 [64, 1152, 384], P('box', None, 'row'), may hold values from -0.1875 to 0.1875
- inv2: bfloat16 [64, 1152, 1152], P('box', None, 'row'), may hold values from -0.1875 to 0.1875
- panel2: bfloat16 [64, 2, 1152, 384], P('box', None, None, 'row'), may hold values from -0.1875 to 0.1875
- near2: int32 [64, 2], P('box'), may hold values from -1 to 63, as said below
Outputs:
- red_one: float32 [512, 64, 128], P('box', None, 'row')
- red_two: float32 [64, 64, 1152], P('box', None, 'row')
- skel_two: float32 [64, 64, 384], P('box', None, 'row')
The draws below stay inside these ranges and needn't reach their ends.
Inputs may be any that keep to these rules, and one draw needn't show every extreme that they name: For each leaf box, skel1 and red1 together hold every number below 320 exactly once. `red1`: see skel1. For each parent box, skel2 and red2 together hold every number below 1536 exactly once. `red2`: see skel2. `near1`: an entry of box b is -1 or another leaf box c with |c // 8 - b // 8| <= 2; a box may be named twice. `near2`: slot 0 of parent q is q - 1 or -1, slot 1 is q + 1 or -1.
All inputs are finite; a program needn't handle non-finite values.
Results may differ from the reference program's by a relative error of at most 0.0046.
Values may be sent and summed in bfloat16 or wider, within the bound.
A program may use at most 64 MiB of HBM per device.

```python
import jax
import jax.numpy as jnp
from jax import lax

S1 = 192
R1 = 128
NDOF = 320
CHILD = 8
S2 = 384
R2 = 1152
NB1 = 8
NB2 = 2
K = 64
NBOX = 512
NPAR = 64


def split_lists(key, boxes, total, keep):
    base = jax.random.fold_in(key, 11)
    keys = jax.random.split(base, boxes)
    orders = jax.vmap(lambda sub: jax.random.permutation(sub, total))(keys)
    orders = orders.astype(jnp.int32)
    return (orders[:, :keep], orders[:, keep:])


def draw_skel1(key, part):
    return split_lists(key, NBOX, NDOF, S1)[0]


def draw_red1(key, part):
    return split_lists(key, NBOX, NDOF, S1)[1]


def draw_skel2(key, part):
    return split_lists(jax.random.fold_in(key, 5), NPAR, CHILD * S1, S2)[0]


def draw_red2(key, part):
    return split_lists(jax.random.fold_in(key, 5), NPAR, CHILD * S1, S2)[1]


def draw_near1(key, part):
    base = jax.random.fold_in(key, 21)
    step_key, keep_key = jax.random.split(base)
    boxes = jnp.arange(NBOX, dtype=jnp.int32)[:, None]
    step = jax.random.randint(step_key, (NBOX, NB1), -2 * CHILD, 3 * CHILD, dtype=jnp.int32)
    target = boxes // CHILD * CHILD + step
    keep = jax.random.randint(keep_key, (NBOX, NB1), 0, 4, dtype=jnp.int32) > 0
    good = keep & (target >= 0) & (target < NBOX) & (target != boxes)
    near = jnp.where(good, target, -1).astype(jnp.int32)
    near = near.at[NBOX - 2, 0].set(NBOX - 1)
    near = near.at[0, NB1 - 1].set(-1)
    return near.astype(jnp.int32)


def draw_near2(key, part):
    base = jax.random.fold_in(key, 31)
    parents = jnp.arange(NPAR, dtype=jnp.int32)[:, None]
    target = parents + jnp.array([[-1, 1]], dtype=jnp.int32)
    keep = jax.random.randint(base, (NPAR, NB2), 0, 4, dtype=jnp.int32) > 0
    good = keep & (target >= 0) & (target < NPAR)
    near = jnp.where(good, target, -1).astype(jnp.int32)
    near = near.at[NPAR - 2, 1].set(NPAR - 1)
    return near.astype(jnp.int32)


def steps_of(key, shape, cuts, low, top_value):
    factor_of = 1.0
    for axis_at, parts in cuts:
        heights = jax.random.uniform(jax.random.fold_in(jax.random.fold_in(key, 6), axis_at), (parts,), jnp.float32, low / len(cuts), top_value / len(cuts))
        factor_of = factor_of * jnp.repeat(jnp.exp(heights), shape[axis_at] // parts).reshape((-1,) + (1,) * (len(shape) - 1 - axis_at))
    return factor_of


def gaussian(stream_key, dims, spread, limit, cuts=(), held_as=jnp.bfloat16):
    gain = steps_of(stream_key, dims, cuts, -0.22, 0.18) if cuts else 1.0
    values = jax.random.normal(stream_key, dims, jnp.float32) * spread * gain
    return jnp.minimum(jnp.maximum(values, -limit), limit).astype(held_as)


def setup_inputs(seed: int = 0) -> dict:
    streams_of = jax.random.split(jax.random.key(seed), 14)
    rhs = gaussian(streams_of[0], (NBOX, K, NDOF), 1.0, 6.0, ((0, 64),), jnp.float32)
    skel1 = draw_skel1(jax.random.fold_in(streams_of[13], 71), 0)
    red1 = draw_red1(jax.random.fold_in(streams_of[13], 71), 0)
    interp1 = gaussian(streams_of[3], (NBOX, R1, S1), R1 ** -0.5, 0.5, ((0, 64), (2, 8)))
    inv1 = gaussian(streams_of[4], (NBOX, R1, R1), R1 ** -0.5, 0.5, ((0, 64), (2, 8)))
    couple1 = gaussian(streams_of[5], (NBOX, NB1, R1, S1), R1 ** -0.5, 0.5, ((0, 64), (3, 8)))
    near1 = draw_near1(jax.random.fold_in(streams_of[13], 71), 0)
    skel2 = draw_skel2(jax.random.fold_in(streams_of[13], 71), 0)
    red2 = draw_red2(jax.random.fold_in(streams_of[13], 71), 0)
    interp2 = gaussian(streams_of[9], (NPAR, R2, S2), R2 ** -0.5, 0.1875, ((0, 64), (2, 8)))
    inv2 = gaussian(streams_of[10], (NPAR, R2, R2), R2 ** -0.5, 0.1875, ((0, 64), (2, 8)))
    panel2 = gaussian(streams_of[11], (NPAR, NB2, R2, S2), R2 ** -0.5, 0.1875, ((0, 64), (3, 8)))
    near2 = draw_near2(jax.random.fold_in(streams_of[13], 71), 0)
    return {"rhs": rhs, "skel1": skel1, "red1": red1, "interp1": interp1, "inv1": inv1, "couple1": couple1, "near1": near1, "skel2": skel2, "red2": red2, "interp2": interp2, "inv2": inv2, "panel2": panel2, "near2": near2}


def pick(values, index):
    return jax.vmap(lambda block, where: block[:, where])(values, index)


def route_sum(updates, near, count):
    targets = jnp.where(near >= 0, near, count).reshape(-1)
    flat = updates.reshape((-1,) + updates.shape[2:])
    summed = jax.ops.segment_sum(flat, targets, num_segments=count + 1)
    return summed[:count]


def reference(rhs, skel1, red1, interp1, inv1, couple1, near1, skel2, red2, interp2, inv2, panel2, near2):
    high = lax.Precision.HIGHEST
    xr1 = pick(rhs, red1).astype(jnp.bfloat16).astype(jnp.float32)
    ys1 = pick(rhs, skel1) - jnp.einsum("bkr,brs->bks", xr1, interp1.astype(jnp.float32), precision=high)
    red_one = jnp.einsum("bkr,brq->bkq", xr1, inv1.astype(jnp.float32), precision=high)
    w1 = red_one.astype(jnp.bfloat16).astype(jnp.float32)
    u1 = jnp.einsum("bkr,bjrs->bjks", w1, couple1.astype(jnp.float32), precision=high)
    z1 = ys1 + route_sum(u1, near1, NBOX)
    parent = z1.reshape(NPAR, CHILD, K, S1).transpose(0, 2, 1, 3).reshape(NPAR, K, CHILD * S1)
    xr2 = pick(parent, red2).astype(jnp.bfloat16).astype(jnp.float32)
    ys2 = pick(parent, skel2) - jnp.einsum("pkr,prs->pks", xr2, interp2.astype(jnp.float32), precision=high)
    red_two = jnp.einsum("pkr,prq->pkq", xr2, inv2.astype(jnp.float32), precision=high)
    u2 = jnp.einsum("pkr,pjrs->pjks", xr2, panel2.astype(jnp.float32), precision=high)
    skel_two = ys2 + route_sum(u2, near2, NPAR)
    return red_one, red_two, skel_two
```

```python
import functools

import jax
import jax.numpy as jnp
from jax import lax
from jax.experimental import pallas as pl
from jax.experimental.pallas import tpu as pltpu
from jax.sharding import PartitionSpec as P

MESH = pl.DeviceIdType.MESH
F32 = jnp.float32
BF16 = jnp.bfloat16
NROW = 8
STEPS = (-2, 2, -1, 1)


def nt(a, b):
    return lax.dot_general(a, b, (((1,), (1,)), ((), ())), preferred_element_type=F32)


def nn(a, b):
    return jnp.dot(a, b, preferred_element_type=F32)


def place(p):
    box = jnp.floor((p + 0.5) * (1.0 / 192.0))
    rest = p - 192.0 * box
    owner = jnp.floor((rest + 0.5) * (1.0 / 24.0))
    half = jnp.where(box >= 4.0, 1.0, 0.0)
    return 768.0 * half + 96.0 * owner + 24.0 * (box - 4.0 * half) + (rest - 24.0 * owner)


def kernel(
    nbox,
    rhs, skel1, red1, interp1, inv1, couple1, near1, skel2, red2, interp2, inv2, panel2, near2,
    out_one, out_two, out_skel,
    v_rhs, v_skel1, v_red1, v_interp1, v_inv1, v_couple, v_near1, v_skel2, v_red2, v_w2, v_near2,
    rhs16, xr, wall, routed, ys, own, box_send, box_recv, parent, w2s, pair_send, pair_recv,
    one_buf, two_buf, skel_buf,
    load_sem, out_sem, a_send, a_recv, b_send, b_recv, c_send, c_recv, d_send, d_recv,
):
    q = lax.axis_index("box")
    r = lax.axis_index("row")

    loads = []
    for source, target in (
        (red1, v_red1), (rhs, v_rhs), (inv1, v_inv1), (skel1, v_skel1), (interp1, v_interp1),
        (near1, v_near1), (couple1, v_couple), (red2, v_red2), (skel2, v_skel2), (near2, v_near2),
        (panel2, v_w2.at[0:96]), (interp2, v_w2.at[96:144]), (inv2, v_w2.at[144:288]),
    ):
        copy = pltpu.make_async_copy(source, target, load_sem.at[len(loads)])
        copy.start()
        loads.append(copy)

    barrier = pltpu.get_barrier_semaphore()
    row_peers = [lax.rem(r + i, NROW) for i in range(1, NROW)]
    box_peers = [lax.rem(q + nbox + step, nbox) for step in STEPS]
    for peer in row_peers:
        pl.semaphore_signal(barrier, inc=1, device_id=(q, peer), device_id_type=MESH)
    for peer in box_peers:
        pl.semaphore_signal(barrier, inc=1, device_id=(peer, r), device_id_type=MESH)

    low = lax.broadcasted_iota(jnp.int32, (1, 128), 1) < 64

    loads[0].wait()
    loads[1].wait()
    loads[2].wait()
    dof = lax.broadcasted_iota(jnp.int32, (320, 128), 0)
    for b in range(4):
        for h in range(2):
            box = b + 4 * h
            onehot = jnp.where(dof == v_red1[box : box + 1, :], 1.0, 0.0).astype(BF16)
            values = v_rhs[box * 64 : box * 64 + 64, :].astype(BF16)
            rhs16[b, h * 64 : h * 64 + 64, :] = values
            xr[b, h * 64 : h * 64 + 64, :] = nn(values, onehot).astype(BF16)
        x = xr[b]
        first = nt(v_inv1[b], x)
        second = nt(v_inv1[b + 4], x)
        one_buf[b * 16 : b * 16 + 16, :] = first[:, 0:64]
        one_buf[b * 16 + 64 : b * 16 + 80, :] = pltpu.roll(second, 64, 1)[:, 0:64]
        wall[b, pl.ds(pl.multiple_of(r * 16, 16), 16), :] = jnp.where(low, first, second).astype(BF16)

    pl.semaphore_wait(barrier, NROW - 1 + len(STEPS))

    def gather_copy(buffer, index, i, send, recv):
        return pltpu.make_async_remote_copy(
            src_ref=buffer.at[index], dst_ref=buffer.at[index],
            send_sem=send.at[i - 1], recv_sem=recv.at[i - 1],
            device_id=(q, row_peers[i - 1]), device_id_type=MESH,
        )

    mine_a = (slice(None), pl.ds(pl.multiple_of(r * 16, 16), 16), slice(None))
    copies_a = [gather_copy(wall, mine_a, i, a_send, a_recv) for i in range(1, NROW)]
    for i in (4, 3, 5, 2, 6, 1, 7):
        copies_a[i - 1].start()

    out_copy_one = pltpu.make_async_copy(one_buf, out_one, out_sem.at[0])
    out_copy_one.start()

    loads[3].wait()
    loads[4].wait()
    dof_lane = lax.broadcasted_iota(jnp.int32, (24, 320), 1).astype(F32)
    pick = (
        lax.broadcasted_iota(jnp.int32, (24, 192), 1)
        == lax.broadcasted_iota(jnp.int32, (24, 192), 0) + r * 24
    )
    for b in range(4):
        parts = []
        for h in range(2):
            box = b + 4 * h
            names = v_skel1[box : box + 1, :].astype(F32)
            column = jnp.sum(jnp.where(pick, names, 0.0), axis=1, keepdims=True)
            onehot = jnp.where(dof_lane == column, 1.0, 0.0).astype(BF16)
            parts.append(nt(onehot, rhs16[b]) - nt(v_interp1[box], xr[b]))
        ys[b * 24 : b * 24 + 24, :] = jnp.where(low, parts[0], parts[1])

    loads[5].wait()
    loads[6].wait()
    names = v_near1[...]
    relative = jnp.where(names < 0, -64, names - 8 * (q - 2)).astype(F32) * 24.0
    lane = lax.broadcasted_iota(jnp.int32, (8, 192), 1).astype(F32)
    slot = jnp.floor((lane + 0.5) * (1.0 / 24.0))
    key = lane - 24.0 * slot
    for j in range(8):
        key = key + jnp.where(slot == float(j), relative[:, j : j + 1], 0.0)
    key = key.astype(jnp.int32)
    row_id = lax.broadcasted_iota(jnp.int32, (960, 192), 0)
    for box in range(8):
        h, b = box // 4, box % 4
        onehot = jnp.where(row_id == key[box : box + 1, :], 1.0, 0.0).astype(BF16)
        routed[h * 960 : h * 960 + 960, b * 128 : b * 128 + 128] = nn(onehot, v_couple[box]).astype(BF16)

    for copy in copies_a:
        copy.wait_recv()

    w = wall[...].reshape(512, 128)
    copies_b = []
    for n, step in enumerate(STEPS + (0,)):
        base = (step + 2) * 192
        top = nn(routed[base : base + 192, :], w)
        bottom = nn(routed[960 + base : 960 + base + 192, :], w)
        keep = jnp.where(low, top[0:96], bottom[96:192])
        turn = jnp.where(low, top[96:192], bottom[0:96])
        total = keep + pltpu.roll(turn, 64, 1)
        if step == 0:
            own[...] = total + ys[...]
        else:
            box_send[n] = total.astype(BF16)
            copy = pltpu.make_async_remote_copy(
                src_ref=box_send.at[n], dst_ref=box_recv.at[n],
                send_sem=b_send.at[n], recv_sem=b_recv.at[n],
                device_id=(box_peers[n], r), device_id_type=MESH,
            )
            copy.start()
            copies_b.append(copy)

    for copy in loads[7:]:
        copy.wait()
    spots = place(v_red2[...].astype(F32)).astype(jnp.int32)
    pick2 = (
        lax.broadcasted_iota(jnp.int32, (48, 384), 1)
        == lax.broadcasted_iota(jnp.int32, (48, 384), 0) + r * 48
    )
    mine = jnp.sum(jnp.where(pick2, place(v_skel2[...].astype(F32)), 0.0), axis=1, keepdims=True)
    valid = jnp.where(v_near2[...] >= 0, 1.0, 0.0)
    valid = (valid[:, 0:1], valid[:, 1:2])
    spot_row = lax.broadcasted_iota(jnp.int32, (256, 1152), 0)
    spot_lane = lax.broadcasted_iota(jnp.int32, (48, 256), 1)
    mine = mine.astype(jnp.int32)

    def scatter(i):
        h, j = i // 3, i % 3
        onehot = jnp.where(spot_row + i * 256 == spots, 1.0, 0.0).astype(BF16)
        moved = nt(v_w2[...], onehot)
        chosen = jnp.where(spot_lane + i * 256 == mine, 1.0, 0.0)
        lanes = slice(j * 256, j * 256 + 256)
        w2s[h * 288 : h * 288 + 48, lanes] = (moved[0:48] * valid[0]).astype(BF16)
        w2s[h * 288 + 48 : h * 288 + 96, lanes] = (moved[48:96] * valid[1]).astype(BF16)
        w2s[h * 288 + 96 : h * 288 + 144, lanes] = (chosen - moved[96:144]).astype(BF16)
        w2s[h * 288 + 144 : h * 288 + 288, lanes] = moved[144:288].astype(BF16)

    for i in range(3):
        scatter(i)

    for copy in copies_b:
        copy.wait_recv()
    z = own[...]
    for n in range(4):
        z = z + box_recv[n].astype(F32)
    rows = pl.ds(pl.multiple_of(r * 96, 16), 96)
    parent[rows, :] = z.astype(BF16)
    copies_c = [gather_copy(parent, (rows, slice(None)), i, c_send, c_recv) for i in range(1, NROW)]
    for i in (4, 3, 5, 2, 6, 1, 7):
        copies_c[i - 1].start()

    for i in range(3, 6):
        scatter(i)

    for copy in copies_c:
        copy.wait_recv()

    p = parent[...]
    pair = nn(w2s[0:96, :], p) + pltpu.roll(nn(w2s[288:384, :], p), 64, 1)
    pair_send[...] = pair.astype(BF16).reshape(2, 48, 128)
    copies_d = []
    for n, step in enumerate((-1, 1)):
        copy = pltpu.make_async_remote_copy(
            src_ref=pair_send.at[n], dst_ref=pair_recv.at[n],
            send_sem=d_send.at[n], recv_sem=d_recv.at[n],
            device_id=(lax.rem(q + nbox + step, nbox), r), device_id_type=MESH,
        )
        copy.start()
        copies_d.append(copy)

    skel = nn(w2s[96:144, :], p) + pltpu.roll(nn(w2s[384:432, :], p), 64, 1)

    def tn(a, b):
        return lax.dot_general(a, b, (((0,), (1,)), ((), ())), preferred_element_type=F32)

    two_buf[...] = tn(p, w2s[144:288, :])[0:64] + tn(p, w2s[432:576, :])[64:128]
    out_copy_two = pltpu.make_async_copy(two_buf, out_two, out_sem.at[1])
    out_copy_two.start()

    for copy in copies_d:
        copy.wait_recv()
    skel = skel + pair_recv[0].astype(F32) + pair_recv[1].astype(F32)
    skel_buf[...] = skel[:, 0:64]
    out_copy_skel = pltpu.make_async_copy(skel_buf, out_skel, out_sem.at[2])
    out_copy_skel.start()
    for copy in copies_a + copies_b + copies_c + copies_d:
        copy.wait_send()
    out_copy_one.wait()
    out_copy_two.wait()
    out_copy_skel.wait()


def shards(nbox, rhs, skel1, red1, interp1, inv1, couple1, near1, skel2, red2, interp2, inv2, panel2, near2):
    turned = lambda a: jnp.swapaxes(a, -1, -2)
    operands = (
        rhs.reshape(512, 320), skel1, red1, turned(interp1), turned(inv1),
        turned(couple1).reshape(8, 192, 128), near1, skel2, red2,
        turned(interp2).reshape(48, 1152), turned(inv2).reshape(144, 1152),
        turned(panel2).reshape(96, 1152), near2,
    )
    dma = pltpu.SemaphoreType.DMA
    one, two, skel = pl.pallas_call(
        functools.partial(kernel, nbox),
        out_shape=(
            jax.ShapeDtypeStruct((128, 64), F32),
            jax.ShapeDtypeStruct((64, 144), F32),
            jax.ShapeDtypeStruct((48, 64), F32),
        ),
        in_specs=[pl.BlockSpec(memory_space=pl.ANY)] * len(operands),
        out_specs=(pl.BlockSpec(memory_space=pl.ANY),) * 3,
        scratch_shapes=[
            pltpu.VMEM((512, 320), F32),
            pltpu.VMEM((8, 192), jnp.int32),
            pltpu.VMEM((8, 128), jnp.int32),
            pltpu.VMEM((8, 24, 128), BF16),
            pltpu.VMEM((8, 16, 128), BF16),
            pltpu.VMEM((8, 192, 128), BF16),
            pltpu.VMEM((8, 8), jnp.int32),
            pltpu.VMEM((1, 384), jnp.int32),
            pltpu.VMEM((1, 1152), jnp.int32),
            pltpu.VMEM((288, 1152), BF16),
            pltpu.VMEM((1, 2), jnp.int32),
            pltpu.VMEM((4, 128, 320), BF16),
            pltpu.VMEM((4, 128, 128), BF16),
            pltpu.VMEM((4, 128, 128), BF16),
            pltpu.VMEM((1920, 512), BF16),
            pltpu.VMEM((96, 128), F32),
            pltpu.VMEM((96, 128), F32),
            pltpu.VMEM((4, 96, 128), BF16),
            pltpu.VMEM((4, 96, 128), BF16),
            pltpu.VMEM((768, 128), BF16),
            pltpu.VMEM((576, 768), BF16),
            pltpu.VMEM((2, 48, 128), BF16),
            pltpu.VMEM((2, 48, 128), BF16),
            pltpu.VMEM((128, 64), F32),
            pltpu.VMEM((64, 144), F32),
            pltpu.VMEM((48, 64), F32),
            dma((13,)), dma((3,)),
            dma((7,)), dma((7,)), dma((4,)), dma((4,)), dma((7,)), dma((7,)), dma((2,)), dma((2,)),
        ],
        compiler_params=pltpu.CompilerParams(
            collective_id=0, has_side_effects=True, vmem_limit_bytes=60 << 20
        ),
        name="skeleton_step",
    )(*operands)
    return (
        jnp.swapaxes(one.reshape(8, 16, 64), 1, 2),
        two.reshape(1, 64, 144),
        jnp.swapaxes(skel.reshape(1, 48, 64), 1, 2),
    )


def solution(mesh):
    return jax.shard_map(
        functools.partial(shards, mesh.shape["box"]),
        mesh=mesh,
        in_specs=(
            P("box", None, None),
            P("box", None),
            P("box", None),
            P("box", None, "row"),
            P("box", None, "row"),
            P("box", None, None, "row"),
            P("box", None),
            P("box", None),
            P("box", None),
            P("box", None, "row"),
            P("box", None, "row"),
            P("box", None, None, "row"),
            P("box", None),
        ),
        out_specs=(P("box", None, "row"), P("box", None, "row"), P("box", None, "row")),
        check_vma=False,
    )
```

```python
import functools

import jax
import jax.numpy as jnp
from jax import lax
from jax.experimental import pallas as pl
from jax.experimental.pallas import tpu as pltpu
from jax.sharding import PartitionSpec as P

MESH = pl.DeviceIdType.MESH
F32 = jnp.float32
BF16 = jnp.bfloat16
NROW = 8
STEPS = (-2, 2, -1, 1)
SHAPES = ((128, 64), (64, 144), (48, 64))


def nt(a, b):
    return lax.dot_general(a, b, (((1,), (1,)), ((), ())), preferred_element_type=F32)


def nn(a, b):
    return jnp.dot(a, b, preferred_element_type=F32)


def inside(q, nbox):
    return jnp.logical_and(q >= 0, q < nbox)


def place(p):
    box = jnp.floor((p + 0.5) * (1.0 / 192.0))
    rest = p - 192.0 * box
    owner = jnp.floor((rest + 0.5) * (1.0 / 24.0))
    half = jnp.where(box >= 4.0, 1.0, 0.0)
    return 768.0 * half + 96.0 * owner + 24.0 * (box - 4.0 * half) + (rest - 24.0 * owner)


def kernel(
    nbox,
    rhs, skel1, red1, interp1, inv1, couple1, near1, skel2, red2, interp2, inv2, panel2, near2,
    one_buf, two_buf, skel_buf,
    v_rhs, v_skel1, v_red1, v_interp1, v_inv1, v_couple, v_near1, v_skel2, v_red2, v_w2, v_near2,
    rhs16, xr, wall, routed, ys, own, box_send, box_recv, parent, w2s, pair_send, pair_recv,
    load_sem, a_send, a_recv, b_send, b_recv, c_send, c_recv, d_send, d_recv,
):
    q = lax.axis_index("box")
    r = lax.axis_index("row")

    loads = []
    for source, target in (
        (red1, v_red1), (rhs, v_rhs), (inv1, v_inv1), (skel1, v_skel1), (interp1, v_interp1),
        (near1, v_near1), (couple1, v_couple), (red2, v_red2), (skel2, v_skel2), (near2, v_near2),
        (panel2, v_w2.at[0:96]), (interp2, v_w2.at[96:144]), (inv2, v_w2.at[144:288]),
    ):
        copy = pltpu.make_async_copy(source, target, load_sem.at[len(loads)])
        copy.start()
        loads.append(copy)

    barrier = pltpu.get_barrier_semaphore()
    row_peers = [lax.rem(r + i, NROW) for i in range(1, NROW)]
    box_peers = [q + step for step in STEPS]
    for peer in row_peers:
        pl.semaphore_signal(barrier, inc=1, device_id=(q, peer), device_id_type=MESH)
    for step, peer in zip(STEPS, box_peers):

        @pl.when(inside(q + step, nbox))
        def _():
            pl.semaphore_signal(barrier, inc=1, device_id=(peer, r), device_id_type=MESH)

    for n, step in enumerate(STEPS):

        @pl.when(jnp.logical_not(inside(q - step, nbox)))
        def _():
            box_recv[n] = jnp.zeros(box_recv.shape[1:], BF16)

    for n, step in enumerate((-1, 1)):

        @pl.when(jnp.logical_not(inside(q - step, nbox)))
        def _():
            pair_recv[n] = jnp.zeros(pair_recv.shape[1:], BF16)

    low = lax.broadcasted_iota(jnp.int32, (1, 128), 1) < 64

    loads[0].wait()
    loads[1].wait()
    loads[2].wait()
    dof = lax.broadcasted_iota(jnp.int32, (320, 128), 0)
    for b in range(4):
        for h in range(2):
            box = b + 4 * h
            onehot = jnp.where(dof == v_red1[box : box + 1, :], 1.0, 0.0).astype(BF16)
            values = v_rhs[box * 64 : box * 64 + 64, :].astype(BF16)
            rhs16[b, h * 64 : h * 64 + 64, :] = values
            xr[b, h * 64 : h * 64 + 64, :] = nn(values, onehot).astype(BF16)
        x = xr[b]
        first = nt(v_inv1[b], x)
        second = nt(v_inv1[b + 4], x)
        one_buf[b * 16 : b * 16 + 16, :] = first[:, 0:64]
        one_buf[b * 16 + 64 : b * 16 + 80, :] = pltpu.roll(second, 64, 1)[:, 0:64]
        wall[b, pl.ds(pl.multiple_of(r * 16, 16), 16), :] = jnp.where(low, first, second).astype(BF16)

    greeted = sum(inside(q + step, nbox).astype(jnp.int32) for step in STEPS)
    pl.semaphore_wait(barrier, NROW - 1 + greeted)

    def gather_copy(buffer, index, i, send, recv):
        return pltpu.make_async_remote_copy(
            src_ref=buffer.at[index], dst_ref=buffer.at[index],
            send_sem=send.at[i - 1], recv_sem=recv.at[i - 1],
            device_id=(q, row_peers[i - 1]), device_id_type=MESH,
        )

    mine_a = (slice(None), pl.ds(pl.multiple_of(r * 16, 16), 16), slice(None))
    copies_a = [gather_copy(wall, mine_a, i, a_send, a_recv) for i in range(1, NROW)]
    for i in (4, 3, 5, 2, 6, 1, 7):
        copies_a[i - 1].start()

    loads[3].wait()
    loads[4].wait()
    dof_lane = lax.broadcasted_iota(jnp.int32, (24, 320), 1).astype(F32)
    pick = (
        lax.broadcasted_iota(jnp.int32, (24, 192), 1)
        == lax.broadcasted_iota(jnp.int32, (24, 192), 0) + r * 24
    )
    for b in range(4):
        parts = []
        for h in range(2):
            box = b + 4 * h
            names = v_skel1[box : box + 1, :].astype(F32)
            column = jnp.sum(jnp.where(pick, names, 0.0), axis=1, keepdims=True)
            onehot = jnp.where(dof_lane == column, 1.0, 0.0).astype(BF16)
            parts.append(nt(onehot, rhs16[b]) - nt(v_interp1[box], xr[b]))
        ys[b * 24 : b * 24 + 24, :] = jnp.where(low, parts[0], parts[1])

    loads[5].wait()
    loads[6].wait()
    names = v_near1[...]
    relative = (names - 8 * (q - 2)).astype(F32)
    group = jnp.floor(relative * 0.125)
    child = relative - 8.0 * group
    spot = jnp.where(group == 0.0, 0.0, 4.0)
    for n, step in enumerate(STEPS):
        spot = jnp.where(group == step + 2.0, float(n), spot)
    half = jnp.floor(child * 0.25)
    quarter = child - 4.0 * half
    chunk = jnp.floor(quarter * 0.5)
    relative = 480.0 * chunk + 96.0 * spot + 48.0 * half + 24.0 * (quarter - 2.0 * chunk)
    relative = jnp.where(names < 0, -64.0, relative)
    lane = lax.broadcasted_iota(jnp.int32, (8, 192), 1).astype(F32)
    slot = jnp.floor((lane + 0.5) * (1.0 / 24.0))
    key = lane - 24.0 * slot
    for j in range(8):
        key = key + jnp.where(slot == float(j), relative[:, j : j + 1], 0.0)
    key = key.astype(jnp.int32)
    row_id = lax.broadcasted_iota(jnp.int32, (960, 192), 0)
    for box in range(8):
        h, b = box // 4, box % 4
        onehot = jnp.where(row_id == key[box : box + 1, :], 1.0, 0.0).astype(BF16)
        routed[h * 960 : h * 960 + 960, b * 128 : b * 128 + 128] = nn(onehot, v_couple[box]).astype(BF16)

    for copy in copies_a:
        copy.wait_recv()

    w = wall[...].reshape(512, 128)

    def updates(start, count):
        top = nn(routed[start : start + 96 * count, :], w)
        bottom = nn(routed[960 + start : 960 + start + 96 * count, :], w)
        totals = []
        for n in range(count):
            a = slice(96 * n, 96 * n + 48)
            b = slice(96 * n + 48, 96 * n + 96)
            keep = jnp.where(low, top[a], bottom[b])
            turn = jnp.where(low, top[b], bottom[a])
            totals.append(keep + pltpu.roll(turn, 64, 1))
        return totals

    def box_copy(n, chunk):
        part = pl.ds(chunk * 48, 48)
        return pltpu.make_async_remote_copy(
            src_ref=box_send.at[n, part], dst_ref=box_recv.at[n, part],
            send_sem=b_send.at[chunk, n], recv_sem=b_recv.at[chunk, n],
            device_id=(box_peers[n], r), device_id_type=MESH,
        )

    for chunk in range(2):
        for n, total in enumerate(updates(480 * chunk, 4)):
            box_send[n, chunk * 48 : chunk * 48 + 48, :] = total.astype(BF16)
        for n, step in enumerate(STEPS):

            @pl.when(inside(q + step, nbox))
            def _():
                box_copy(n, chunk).start()

    for chunk in range(2):
        part = slice(chunk * 48, chunk * 48 + 48)
        own[part, :] = updates(480 * chunk + 384, 1)[0] + ys[part, :]

    for copy in loads[7:]:
        copy.wait()
    spots = place(v_red2[...].astype(F32)).astype(jnp.int32)
    pick2 = (
        lax.broadcasted_iota(jnp.int32, (48, 384), 1)
        == lax.broadcasted_iota(jnp.int32, (48, 384), 0) + r * 48
    )
    mine = jnp.sum(jnp.where(pick2, place(v_skel2[...].astype(F32)), 0.0), axis=1, keepdims=True)
    valid = jnp.where(v_near2[...] >= 0, 1.0, 0.0)
    valid = (valid[:, 0:1], valid[:, 1:2])
    spot_row = lax.broadcasted_iota(jnp.int32, (256, 1152), 0)
    spot_lane = lax.broadcasted_iota(jnp.int32, (48, 256), 1)
    mine = mine.astype(jnp.int32)

    def scatter(i):
        h, j = i // 3, i % 3
        onehot = jnp.where(spot_row + i * 256 == spots, 1.0, 0.0).astype(BF16)
        moved = nt(v_w2[...], onehot)
        chosen = jnp.where(spot_lane + i * 256 == mine, 1.0, 0.0)
        lanes = slice(j * 256, j * 256 + 256)
        w2s[h * 288 : h * 288 + 48, lanes] = (moved[0:48] * valid[0]).astype(BF16)
        w2s[h * 288 + 48 : h * 288 + 96, lanes] = (moved[48:96] * valid[1]).astype(BF16)
        w2s[h * 288 + 96 : h * 288 + 144, lanes] = (chosen - moved[96:144]).astype(BF16)
        w2s[h * 288 + 144 : h * 288 + 288, lanes] = moved[144:288].astype(BF16)

    for i in range(3):
        scatter(i)

    copies_c = []
    for chunk in range(2):
        for n, step in enumerate(STEPS):

            @pl.when(inside(q - step, nbox))
            def _():
                box_copy(n, chunk).wait_recv()

        part = slice(chunk * 48, chunk * 48 + 48)
        z = own[part, :]
        for n in range(4):
            z = z + box_recv[n, part, :].astype(F32)
        rows = pl.ds(pl.multiple_of(r * 96 + chunk * 48, 16), 48)
        parent[rows, :] = z.astype(BF16)
        for i in (4, 3, 5, 2, 6, 1, 7):
            copies_c.append(gather_copy(parent, (rows, slice(None)), i, c_send.at[chunk], c_recv.at[chunk]))
            copies_c[-1].start()

    for i in range(3, 6):
        scatter(i)

    for copy in copies_c:
        copy.wait_recv()

    p = parent[...]
    pair = nn(w2s[0:96, :], p) + pltpu.roll(nn(w2s[288:384, :], p), 64, 1)
    pair_send[...] = pair.astype(BF16).reshape(2, 48, 128)
    def pair_copy(n, step):
        return pltpu.make_async_remote_copy(
            src_ref=pair_send.at[n], dst_ref=pair_recv.at[n],
            send_sem=d_send.at[n], recv_sem=d_recv.at[n],
            device_id=(q + step, r), device_id_type=MESH,
        )

    for n, step in enumerate((-1, 1)):

        @pl.when(inside(q + step, nbox))
        def _():
            pair_copy(n, step).start()

    skel = nn(w2s[96:144, :], p) + pltpu.roll(nn(w2s[384:432, :], p), 64, 1)

    def tn(a, b):
        return lax.dot_general(a, b, (((0,), (1,)), ((), ())), preferred_element_type=F32)

    two_buf[...] = tn(p, w2s[144:288, :])[0:64] + tn(p, w2s[432:576, :])[64:128]

    for n, step in enumerate((-1, 1)):

        @pl.when(inside(q - step, nbox))
        def _():
            pair_copy(n, step).wait_recv()

    skel = skel + pair_recv[0].astype(F32) + pair_recv[1].astype(F32)
    skel_buf[...] = skel[:, 0:64]
    for n, step in enumerate(STEPS):

        @pl.when(inside(q + step, nbox))
        def _():
            box_copy(n, 0).wait_send()
            box_copy(n, 1).wait_send()

    for n, step in enumerate((-1, 1)):

        @pl.when(inside(q + step, nbox))
        def _():
            pair_copy(n, step).wait_send()

    for copy in copies_a + copies_c:
        copy.wait_send()


def finish(one, two, skel, out_one, out_two, out_skel, sem):
    copies = [
        pltpu.make_async_copy(source, target, sem.at[n])
        for n, (source, target) in enumerate(((one, out_one), (two, out_two), (skel, out_skel)))
    ]
    for copy in copies:
        copy.start()
    for copy in copies:
        copy.wait()


def shards(nbox, rhs, skel1, red1, interp1, inv1, couple1, near1, skel2, red2, interp2, inv2, panel2, near2):
    turned = lambda a: jnp.swapaxes(a, -1, -2)
    operands = (
        rhs.reshape(512, 320), skel1, red1, turned(interp1), turned(inv1),
        turned(couple1).reshape(8, 192, 128), near1, skel2, red2,
        turned(interp2).reshape(48, 1152), turned(inv2).reshape(144, 1152),
        turned(panel2).reshape(96, 1152), near2,
    )
    dma = pltpu.SemaphoreType.DMA
    one, two, skel = pl.pallas_call(
        functools.partial(kernel, nbox),
        out_shape=tuple(pltpu.VMEM(shape, F32) for shape in SHAPES),
        in_specs=[pl.BlockSpec(memory_space=pl.ANY)] * len(operands),
        out_specs=(pl.BlockSpec(memory_space=pltpu.VMEM),) * 3,
        scratch_shapes=[
            pltpu.VMEM((512, 320), F32),
            pltpu.VMEM((8, 192), jnp.int32),
            pltpu.VMEM((8, 128), jnp.int32),
            pltpu.VMEM((8, 24, 128), BF16),
            pltpu.VMEM((8, 16, 128), BF16),
            pltpu.VMEM((8, 192, 128), BF16),
            pltpu.VMEM((8, 8), jnp.int32),
            pltpu.VMEM((1, 384), jnp.int32),
            pltpu.VMEM((1, 1152), jnp.int32),
            pltpu.VMEM((288, 1152), BF16),
            pltpu.VMEM((1, 2), jnp.int32),
            pltpu.VMEM((4, 128, 320), BF16),
            pltpu.VMEM((4, 128, 128), BF16),
            pltpu.VMEM((4, 128, 128), BF16),
            pltpu.VMEM((1920, 512), BF16),
            pltpu.VMEM((96, 128), F32),
            pltpu.VMEM((96, 128), F32),
            pltpu.VMEM((4, 96, 128), BF16),
            pltpu.VMEM((4, 96, 128), BF16),
            pltpu.VMEM((768, 128), BF16),
            pltpu.VMEM((576, 768), BF16),
            pltpu.VMEM((2, 48, 128), BF16),
            pltpu.VMEM((2, 48, 128), BF16),
            dma((13,)),
            dma((7,)), dma((7,)), dma((2, 4)), dma((2, 4)), dma((2, 7)), dma((2, 7)), dma((2,)), dma((2,)),
        ],
        compiler_params=pltpu.CompilerParams(
            collective_id=0, has_side_effects=True, vmem_limit_bytes=60 << 20
        ),
        name="skeleton_step",
    )(*operands)
    one, two, skel = pl.pallas_call(
        finish,
        out_shape=tuple(jax.ShapeDtypeStruct(shape, F32) for shape in SHAPES),
        in_specs=[pl.BlockSpec(memory_space=pltpu.VMEM)] * 3,
        out_specs=(pl.BlockSpec(memory_space=pl.ANY),) * 3,
        scratch_shapes=[dma((3,))],
        name="write_results",
    )(*(pltpu.with_memory_space_constraint(a, pltpu.VMEM) for a in (one, two, skel)))
    return (
        jnp.swapaxes(one.reshape(8, 16, 64), 1, 2),
        two.reshape(1, 64, 144),
        jnp.swapaxes(skel.reshape(1, 48, 64), 1, 2),
    )


def solution(mesh):
    return jax.shard_map(
        functools.partial(shards, mesh.shape["box"]),
        mesh=mesh,
        in_specs=(
            P("box", None, None),
            P("box", None),
            P("box", None),
            P("box", None, "row"),
            P("box", None, "row"),
            P("box", None, None, "row"),
            P("box", None),
            P("box", None),
            P("box", None),
            P("box", None, "row"),
            P("box", None, "row"),
            P("box", None, None, "row"),
            P("box", None),
        ),
        out_specs=(P("box", None, "row"), P("box", None, "row"), P("box", None, "row")),
        check_vma=False,
    )
```

```python
import functools

import jax
import jax.numpy as jnp
from jax import lax
from jax.experimental import pallas as pl
from jax.experimental.pallas import tpu as pltpu
from jax.sharding import PartitionSpec as P

MESH = pl.DeviceIdType.MESH
F32 = jnp.float32
BF16 = jnp.bfloat16
NROW = 8
STEPS = (-2, 2, -1, 1)
SHAPES = ((128, 64), (64, 144), (48, 64))


def nt(a, b):
    return lax.dot_general(a, b, (((1,), (1,)), ((), ())), preferred_element_type=F32)


def nn(a, b):
    return jnp.dot(a, b, preferred_element_type=F32)


def inside(q, nbox):
    return jnp.logical_and(q >= 0, q < nbox)


def place(p, stride):
    box = jnp.floor((p + 0.5) * (1.0 / 192.0))
    rest = p - 192.0 * box
    owner = jnp.floor((rest + 0.5) * (1.0 / 24.0))
    half = jnp.where(box >= 4.0, 1.0, 0.0)
    return stride * (8.0 * half + owner) + 24.0 * (box - 4.0 * half) + (rest - 24.0 * owner)


def kernel(
    nbox,
    rhs, skel1, red1, interp1, inv1, couple1, near1, skel2, red2, interp2, inv2, panel2, near2,
    one_buf, two_buf, skel_buf,
    v_rhs, v_skel1, v_red1, v_interp1, v_inv1, v_couple, v_near1, v_skel2, v_red2, v_w2, v_near2,
    rhs16, xr, wall, routed, ys, own, box_send, box_recv, parent, w2s, pair_send, pair_recv,
    load_sem, a_send, a_recv, b_send, b_recv, c_send, c_recv, d_send, d_recv,
    deal_send, deal_recv, w_send, w_recv, ready,
):
    q = lax.axis_index("box")
    r = lax.axis_index("row")

    loads = []
    for source, target in (
        (red1, v_red1), (rhs, v_rhs), (inv1, v_inv1), (skel1, v_skel1), (interp1, v_interp1),
        (near1, v_near1), (couple1, v_couple), (red2, v_red2), (skel2, v_skel2), (near2, v_near2),
        (panel2, v_w2.at[0:96]), (interp2, v_w2.at[96:144]), (inv2, v_w2.at[144:288]),
    ):
        copy = pltpu.make_async_copy(source, target, load_sem.at[len(loads)])
        copy.start()
        loads.append(copy)

    barrier = pltpu.get_barrier_semaphore()
    row_peers = [lax.rem(r + i, NROW) for i in range(1, NROW)]
    box_peers = [q + step for step in STEPS]
    for peer in row_peers:
        pl.semaphore_signal(barrier, inc=1, device_id=(q, peer), device_id_type=MESH)
    for n, step in enumerate((-1, 1)):

        @pl.when(inside(q + step, nbox))
        def _():
            pl.semaphore_signal(barrier, inc=1, device_id=(q + step, r), device_id_type=MESH)

    for n, step in enumerate(STEPS):

        @pl.when(jnp.logical_not(inside(q - step, nbox)))
        def _():
            box_recv[n] = jnp.zeros(box_recv.shape[1:], BF16)

    for n, step in enumerate((-1, 1)):

        @pl.when(jnp.logical_not(inside(q - step, nbox)))
        def _():
            pair_recv[n] = jnp.zeros(pair_recv.shape[1:], BF16)

    low = lax.broadcasted_iota(jnp.int32, (1, 128), 1) < 64

    loads[0].wait()
    loads[1].wait()
    loads[2].wait()
    dof = lax.broadcasted_iota(jnp.int32, (320, 128), 0)
    for b in range(4):
        for h in range(2):
            box = b + 4 * h
            onehot = jnp.where(dof == v_red1[box : box + 1, :], 1.0, 0.0).astype(BF16)
            values = v_rhs[box * 64 : box * 64 + 64, :].astype(BF16)
            rhs16[b, h * 64 : h * 64 + 64, :] = values
            xr[b, h * 64 : h * 64 + 64, :] = nn(values, onehot).astype(BF16)
        x = xr[b]
        first = nt(v_inv1[b], x)
        second = nt(v_inv1[b + 4], x)
        one_buf[b * 16 : b * 16 + 16, :] = first[:, 0:64]
        one_buf[b * 16 + 64 : b * 16 + 80, :] = pltpu.roll(second, 64, 1)[:, 0:64]
        wall[b, pl.ds(pl.multiple_of(r * 16, 16), 16), :] = jnp.where(low, first, second).astype(BF16)

    greeted = sum(inside(q + step, nbox).astype(jnp.int32) for step in (-1, 1))
    pl.semaphore_wait(barrier, NROW - 1 + greeted)

    for n, step in enumerate((-1, 1)):

        @pl.when(inside(q + step, nbox))
        def _():
            pl.semaphore_signal(ready.at[n], inc=1, device_id=(q + step, r), device_id_type=MESH)

    def gather_copy(buffer, index, i, send, recv):
        return pltpu.make_async_remote_copy(
            src_ref=buffer.at[index], dst_ref=buffer.at[index],
            send_sem=send.at[i - 1], recv_sem=recv.at[i - 1],
            device_id=(q, row_peers[i - 1]), device_id_type=MESH,
        )

    mine_a = (slice(None), pl.ds(pl.multiple_of(r * 16, 16), 16), slice(None))
    copies_a = [gather_copy(wall, mine_a, i, a_send, a_recv) for i in range(1, NROW)]
    for i in (4, 3, 5, 2, 6, 1, 7):
        copies_a[i - 1].start()

    for n in (7, 9, 10):
        loads[n].wait()
    spots = place(v_red2[...].astype(F32), 128.0).astype(jnp.int32)
    spot_row = lax.broadcasted_iota(jnp.int32, (256, 1152), 0)
    valid = jnp.where(v_near2[...] >= 0, 1.0, 0.0)
    valid = (valid[:, 0:1], valid[:, 1:2])
    for i in range(8):
        onehot = jnp.where(spot_row + i * 256 == spots, 1.0, 0.0).astype(BF16)
        moved = nt(v_w2[0:96, :], onehot)
        for n in range(2):
            d, h = (2 * i + n) % 8, i // 4
            lanes = slice(n * 128, n * 128 + 128)
            deal_send[d, h * 96 : h * 96 + 48, :] = (moved[0:48, lanes] * valid[0]).astype(BF16)
            deal_send[d, h * 96 + 48 : h * 96 + 96, :] = (moved[48:96, lanes] * valid[1]).astype(BF16)
    deal_recv[r] = deal_send[r]
    copies_w = []
    for i in (4, 3, 5, 2, 6, 1, 7):
        copy = pltpu.make_async_remote_copy(
            src_ref=deal_send.at[row_peers[i - 1]], dst_ref=deal_recv.at[r],
            send_sem=w_send.at[i - 1], recv_sem=w_recv.at[i - 1],
            device_id=(q, row_peers[i - 1]), device_id_type=MESH,
        )
        copy.start()
        copies_w.append(copy)

    loads[3].wait()
    loads[4].wait()
    dof_lane = lax.broadcasted_iota(jnp.int32, (24, 320), 1).astype(F32)
    pick = (
        lax.broadcasted_iota(jnp.int32, (24, 192), 1)
        == lax.broadcasted_iota(jnp.int32, (24, 192), 0) + r * 24
    )
    for b in range(4):
        parts = []
        for h in range(2):
            box = b + 4 * h
            names = v_skel1[box : box + 1, :].astype(F32)
            column = jnp.sum(jnp.where(pick, names, 0.0), axis=1, keepdims=True)
            onehot = jnp.where(dof_lane == column, 1.0, 0.0).astype(BF16)
            parts.append(nt(onehot, rhs16[b]) - nt(v_interp1[box], xr[b]))
        ys[b * 24 : b * 24 + 24, :] = jnp.where(low, parts[0], parts[1])

    loads[5].wait()
    loads[6].wait()
    names = v_near1[...]
    relative = (names - 8 * (q - 2)).astype(F32)
    group = jnp.floor(relative * 0.125)
    child = relative - 8.0 * group
    spot = jnp.where(group == 0.0, 0.0, 4.0)
    for n, step in enumerate(STEPS):
        spot = jnp.where(group == step + 2.0, float(n), spot)
    half = jnp.floor(child * 0.25)
    quarter = child - 4.0 * half
    chunk = jnp.floor(quarter * 0.5)
    relative = 480.0 * chunk + 96.0 * spot + 48.0 * half + 24.0 * (quarter - 2.0 * chunk)
    relative = jnp.where(names < 0, -64.0, relative)
    lane = lax.broadcasted_iota(jnp.int32, (8, 192), 1).astype(F32)
    slot = jnp.floor((lane + 0.5) * (1.0 / 24.0))
    key = lane - 24.0 * slot
    for j in range(8):
        key = key + jnp.where(slot == float(j), relative[:, j : j + 1], 0.0)
    key = key.astype(jnp.int32)
    row_id = lax.broadcasted_iota(jnp.int32, (960, 192), 0)
    for box in range(8):
        h, b = box // 4, box % 4
        onehot = jnp.where(row_id == key[box : box + 1, :], 1.0, 0.0).astype(BF16)
        routed[h * 960 : h * 960 + 960, b * 128 : b * 128 + 128] = nn(onehot, v_couple[box]).astype(BF16)

    for copy in copies_a:
        copy.wait_recv()

    w = wall[...].reshape(512, 128)

    def updates(start, count):
        top = nn(routed[start : start + 96 * count, :], w)
        bottom = nn(routed[960 + start : 960 + start + 96 * count, :], w)
        totals = []
        for n in range(count):
            a = slice(96 * n, 96 * n + 48)
            b = slice(96 * n + 48, 96 * n + 96)
            keep = jnp.where(low, top[a], bottom[b])
            turn = jnp.where(low, top[b], bottom[a])
            totals.append(keep + pltpu.roll(turn, 64, 1))
        return totals

    def box_copy(n, chunk):
        part = pl.ds(chunk * 48, 48)
        return pltpu.make_async_remote_copy(
            src_ref=box_send.at[n, part], dst_ref=box_recv.at[n, part],
            send_sem=b_send.at[chunk, n], recv_sem=b_recv.at[chunk, n],
            device_id=(box_peers[n], r), device_id_type=MESH,
        )

    for n, step in enumerate((-1, 1)):

        @pl.when(inside(q - step, nbox))
        def _():
            pl.semaphore_wait(ready.at[n], 1)

    for chunk in range(2):
        for n, total in enumerate(updates(480 * chunk, 4)):
            box_send[n, chunk * 48 : chunk * 48 + 48, :] = total.astype(BF16)
        for n, step in enumerate(STEPS):

            @pl.when(inside(q + step, nbox))
            def _():
                box_copy(n, chunk).start()

    for chunk in range(2):
        part = slice(chunk * 48, chunk * 48 + 48)
        own[part, :] = updates(480 * chunk + 384, 1)[0] + ys[part, :]

    for n in (8, 11, 12):
        loads[n].wait()
    spots = place(v_red2[...].astype(F32), 96.0).astype(jnp.int32)
    pick2 = (
        lax.broadcasted_iota(jnp.int32, (48, 384), 1)
        == lax.broadcasted_iota(jnp.int32, (48, 384), 0) + r * 48
    )
    mine = jnp.sum(jnp.where(pick2, place(v_skel2[...].astype(F32), 96.0), 0.0), axis=1, keepdims=True)
    spot_lane = lax.broadcasted_iota(jnp.int32, (48, 256), 1)
    mine = mine.astype(jnp.int32)

    def scatter(i):
        h, j = i // 3, i % 3
        onehot = jnp.where(spot_row + i * 256 == spots, 1.0, 0.0).astype(BF16)
        moved = nt(v_w2[96:288, :], onehot)
        chosen = jnp.where(spot_lane + i * 256 == mine, 1.0, 0.0)
        lanes = slice(j * 256, j * 256 + 256)
        w2s[h * 192 : h * 192 + 48, lanes] = (chosen - moved[0:48]).astype(BF16)
        w2s[h * 192 + 48 : h * 192 + 192, lanes] = moved[48:192].astype(BF16)

    for i in range(3):
        scatter(i)

    copies_c = []
    for chunk in range(2):
        for n, step in enumerate(STEPS):

            @pl.when(inside(q - step, nbox))
            def _():
                box_copy(n, chunk).wait_recv()

        part = slice(chunk * 48, chunk * 48 + 48)
        z = own[part, :]
        for n in range(4):
            z = z + box_recv[n, part, :].astype(F32)
        rows = pl.ds(pl.multiple_of(r * 96 + chunk * 48, 16), 48)
        parent[rows, :] = z.astype(BF16)
        for i in (4, 3, 5, 2, 6, 1, 7):
            copies_c.append(gather_copy(parent, (rows, slice(None)), i, c_send.at[chunk], c_recv.at[chunk]))
            copies_c[-1].start()

    for copy in copies_w:
        copy.wait_recv()
    block = parent[pl.ds(pl.multiple_of(r * 96, 16), 96), :]

    def pair_copy(n, step, row):
        return pltpu.make_async_remote_copy(
            src_ref=pair_send.at[n, row], dst_ref=pair_recv.at[n, r],
            send_sem=d_send.at[n, row], recv_sem=d_recv.at[n, r],
            device_id=(q + step, row), device_id_type=MESH,
        )

    def pair_arrival(n, row):
        return pltpu.make_async_remote_copy(
            src_ref=pair_send.at[n, row], dst_ref=pair_recv.at[n, row],
            send_sem=d_send.at[n, row], recv_sem=d_recv.at[n, row],
            device_id=(q, row), device_id_type=MESH,
        )

    deal = nn(deal_recv[...].reshape(1536, 128)[:, 0:96], block)
    for row in range(NROW):
        for n in range(2):
            a = row * 192 + n * 48
            b = a + 96
            keep = jnp.where(low, deal[a : a + 24], deal[b + 24 : b + 48])
            turn = jnp.where(low, deal[a + 24 : a + 48], deal[b : b + 24])
            pair_send[n, row] = (keep + pltpu.roll(turn, 64, 1)).astype(BF16)
    for n, step in enumerate((-1, 1)):

        @pl.when(inside(q + step, nbox))
        def _():
            for row in range(NROW):
                pair_copy(n, step, row).start()

    for i in range(3, 6):
        scatter(i)

    for copy in copies_c:
        copy.wait_recv()

    p = parent[...]
    skel = nn(w2s[0:48, :], p) + pltpu.roll(nn(w2s[192:240, :], p), 64, 1)

    def tn(a, b):
        return lax.dot_general(a, b, (((0,), (1,)), ((), ())), preferred_element_type=F32)

    two_buf[...] = tn(p, w2s[48:192, :])[0:64] + tn(p, w2s[240:384, :])[64:128]

    for n, step in enumerate((-1, 1)):

        @pl.when(inside(q - step, nbox))
        def _():
            for row in range(NROW):
                pair_arrival(n, row).wait_recv()

    pairs = jnp.sum(pair_recv[...].astype(F32).reshape(16, 24, 128), axis=0)
    skel_buf[0:24, :] = (skel[0:24] + pairs)[:, 0:64]
    skel_buf[24:48, :] = (skel[24:48] + pltpu.roll(pairs, 64, 1))[:, 0:64]
    for n, step in enumerate(STEPS):

        @pl.when(inside(q + step, nbox))
        def _():
            box_copy(n, 0).wait_send()
            box_copy(n, 1).wait_send()

    for n, step in enumerate((-1, 1)):

        @pl.when(inside(q + step, nbox))
        def _():
            for row in range(NROW):
                pair_copy(n, step, row).wait_send()

    for copy in copies_a + copies_w + copies_c:
        copy.wait_send()


def finish(one, two, skel, out_one, out_two, out_skel, sem):
    copies = [
        pltpu.make_async_copy(source, target, sem.at[n])
        for n, (source, target) in enumerate(((one, out_one), (two, out_two), (skel, out_skel)))
    ]
    for copy in copies:
        copy.start()
    for copy in copies:
        copy.wait()


def shards(nbox, rhs, skel1, red1, interp1, inv1, couple1, near1, skel2, red2, interp2, inv2, panel2, near2):
    turned = lambda a: jnp.swapaxes(a, -1, -2)
    operands = (
        rhs.reshape(512, 320), skel1, red1, turned(interp1), turned(inv1),
        turned(couple1).reshape(8, 192, 128), near1, skel2, red2,
        turned(interp2).reshape(48, 1152), turned(inv2).reshape(144, 1152),
        turned(panel2).reshape(96, 1152), near2,
    )
    dma = pltpu.SemaphoreType.DMA
    one, two, skel = pl.pallas_call(
        functools.partial(kernel, nbox),
        out_shape=tuple(pltpu.VMEM(shape, F32) for shape in SHAPES),
        in_specs=[pl.BlockSpec(memory_space=pl.ANY)] * len(operands),
        out_specs=(pl.BlockSpec(memory_space=pltpu.VMEM),) * 3,
        scratch_shapes=[
            pltpu.VMEM((512, 320), F32),
            pltpu.VMEM((8, 192), jnp.int32),
            pltpu.VMEM((8, 128), jnp.int32),
            pltpu.VMEM((8, 24, 128), BF16),
            pltpu.VMEM((8, 16, 128), BF16),
            pltpu.VMEM((8, 192, 128), BF16),
            pltpu.VMEM((8, 8), jnp.int32),
            pltpu.VMEM((1, 384), jnp.int32),
            pltpu.VMEM((1, 1152), jnp.int32),
            pltpu.VMEM((288, 1152), BF16),
            pltpu.VMEM((1, 2), jnp.int32),
            pltpu.VMEM((4, 128, 320), BF16),
            pltpu.VMEM((4, 128, 128), BF16),
            pltpu.VMEM((4, 128, 128), BF16),
            pltpu.VMEM((1920, 512), BF16),
            pltpu.VMEM((96, 128), F32),
            pltpu.VMEM((96, 128), F32),
            pltpu.VMEM((4, 96, 128), BF16),
            pltpu.VMEM((4, 96, 128), BF16),
            pltpu.VMEM((768, 128), BF16),
            pltpu.VMEM((384, 768), BF16),
            pltpu.VMEM((2, NROW, 24, 128), BF16),
            pltpu.VMEM((2, NROW, 24, 128), BF16),
            dma((13,)),
            dma((7,)), dma((7,)), dma((2, 4)), dma((2, 4)), dma((2, 7)), dma((2, 7)), dma((2, 8)), dma((2, 8)),
            pltpu.VMEM((NROW, 192, 128), BF16),
            pltpu.VMEM((NROW, 192, 128), BF16),
            dma((7,)), dma((7,)), pltpu.SemaphoreType.REGULAR((2,)),
        ],
        compiler_params=pltpu.CompilerParams(
            collective_id=0, has_side_effects=True, vmem_limit_bytes=60 << 20
        ),
        name="skeleton_step",
    )(*operands)
    one, two, skel = pl.pallas_call(
        finish,
        out_shape=tuple(jax.ShapeDtypeStruct(shape, F32) for shape in SHAPES),
        in_specs=[pl.BlockSpec(memory_space=pltpu.VMEM)] * 3,
        out_specs=(pl.BlockSpec(memory_space=pl.ANY),) * 3,
        scratch_shapes=[dma((3,))],
        name="write_results",
    )(*(pltpu.with_memory_space_constraint(a, pltpu.VMEM) for a in (one, two, skel)))
    return (
        jnp.swapaxes(one.reshape(8, 16, 64), 1, 2),
        two.reshape(1, 64, 144),
        jnp.swapaxes(skel.reshape(1, 48, 64), 1, 2),
    )


def solution(mesh):
    return jax.shard_map(
        functools.partial(shards, mesh.shape["box"]),
        mesh=mesh,
        in_specs=(
            P("box", None, None),
            P("box", None),
            P("box", None),
            P("box", None, "row"),
            P("box", None, "row"),
            P("box", None, None, "row"),
            P("box", None),
            P("box", None),
            P("box", None),
            P("box", None, "row"),
            P("box", None, "row"),
            P("box", None, None, "row"),
            P("box", None),
        ),
        out_specs=(P("box", None, "row"), P("box", None, "row"), P("box", None, "row")),
        check_vma=False,
    )
```

```python
import functools

import jax
import jax.numpy as jnp
from jax import lax
from jax.experimental import pallas as pl
from jax.experimental.pallas import tpu as pltpu
from jax.sharding import PartitionSpec as P

MESH = pl.DeviceIdType.MESH
F32 = jnp.float32
BF16 = jnp.bfloat16
NROW = 8
STEPS = (-2, 2, -1, 1)
SHAPES = ((128, 64), (64, 144), (48, 64))


def nt(a, b):
    return lax.dot_general(a, b, (((1,), (1,)), ((), ())), preferred_element_type=F32)


def nn(a, b):
    return jnp.dot(a, b, preferred_element_type=F32)


def one_hot(targets, start, rows, twice=None):
    shift = targets - float(start)
    shift = jnp.where(shift < float(rows), shift, -1.0).astype(BF16)
    row = lax.broadcasted_iota(jnp.int32, (rows, targets.shape[1]), 0)
    if twice is not None:
        row = jnp.where(row < twice, row, row - (rows - twice))
    row = row.astype(F32).astype(BF16)
    return jnp.where(row == shift, jnp.ones((), BF16), jnp.zeros((), BF16))


def inside(q, nbox):
    return jnp.logical_and(q >= 0, q < nbox)


def place(p, stride, halves):
    box = jnp.floor((p + 0.5) * (1.0 / 192.0))
    rest = p - 192.0 * box
    owner = jnp.floor((rest + 0.5) * (1.0 / 24.0))
    half = jnp.where(box >= 4.0, 1.0, 0.0)
    return stride * owner + halves * half + 24.0 * (box - 4.0 * half) + (rest - 24.0 * owner)


def kernel(
    nbox,
    rhs, skel1, red1, interp1, inv1, couple1, near1, skel2, red2, interp2, inv2, panel2, near2,
    one_buf, two_buf, skel_buf,
    v_rhs, v_skel1, v_red1, v_interp1, v_inv1, v_couple, v_near1, v_skel2, v_red2, v_w2, v_near2,
    rhs16, xr, wall, routed, ys, own, box_send, box_recv, parent, w2s, pair_send, pair_recv,
    load_sem, a_send, a_recv, b_send, b_recv, c_send, c_recv, d_send, d_recv,
    deal_send, deal_recv, deal_rest, w_send, w_recv, ready,
):
    q = lax.axis_index("box")
    r = lax.axis_index("row")

    loads = []
    for source, target in (
        (red1, v_red1), (rhs, v_rhs), (inv1, v_inv1), (skel1, v_skel1), (interp1, v_interp1),
        (near1, v_near1), (couple1, v_couple), (red2, v_red2), (skel2, v_skel2), (near2, v_near2),
        (panel2, v_w2.at[0:96]), (interp2, v_w2.at[96:144]), (inv2, v_w2.at[144:288]),
    ):
        copy = pltpu.make_async_copy(source, target, load_sem.at[len(loads)])
        copy.start()
        loads.append(copy)

    barrier = pltpu.get_barrier_semaphore()
    row_peers = [lax.rem(r + i, NROW) for i in range(1, NROW)]
    box_peers = [q + step for step in STEPS]
    for peer in row_peers:
        pl.semaphore_signal(barrier, inc=1, device_id=(q, peer), device_id_type=MESH)
    for n, step in enumerate((-1, 1)):

        @pl.when(inside(q + step, nbox))
        def _():
            pl.semaphore_signal(barrier, inc=1, device_id=(q + step, r), device_id_type=MESH)

    for n, step in enumerate(STEPS):

        @pl.when(jnp.logical_not(inside(q - step, nbox)))
        def _():
            box_recv[n] = jnp.zeros(box_recv.shape[1:], BF16)

    for n, step in enumerate((-1, 1)):

        @pl.when(jnp.logical_not(inside(q - step, nbox)))
        def _():
            pair_recv[n] = jnp.zeros(pair_recv.shape[1:], BF16)

    low = lax.broadcasted_iota(jnp.int32, (1, 128), 1) < 64

    loads[0].wait()
    loads[1].wait()
    loads[2].wait()
    dof = lax.broadcasted_iota(jnp.int32, (320, 128), 0)
    for b in range(4):
        for h in range(2):
            box = b + 4 * h
            onehot = jnp.where(dof == v_red1[box : box + 1, :], 1.0, 0.0).astype(BF16)
            values = v_rhs[box * 64 : box * 64 + 64, :].astype(BF16)
            rhs16[b, h * 64 : h * 64 + 64, :] = values
            xr[b, h * 64 : h * 64 + 64, :] = nn(values, onehot).astype(BF16)
        x = xr[b]
        first = nt(v_inv1[b], x)
        second = nt(v_inv1[b + 4], x)
        one_buf[b * 16 : b * 16 + 16, :] = first[:, 0:64]
        one_buf[b * 16 + 64 : b * 16 + 80, :] = pltpu.roll(second, 64, 1)[:, 0:64]
        wall[b, pl.ds(pl.multiple_of(r * 16, 16), 16), :] = jnp.where(low, first, second).astype(BF16)

    greeted = sum(inside(q + step, nbox).astype(jnp.int32) for step in (-1, 1))
    pl.semaphore_wait(barrier, NROW - 1 + greeted)

    for n, step in enumerate((-1, 1)):

        @pl.when(inside(q + step, nbox))
        def _():
            pl.semaphore_signal(ready.at[n], inc=1, device_id=(q + step, r), device_id_type=MESH)

    def gather_copy(buffer, index, i, send, recv):
        return pltpu.make_async_remote_copy(
            src_ref=buffer.at[index], dst_ref=buffer.at[index],
            send_sem=send.at[i - 1], recv_sem=recv.at[i - 1],
            device_id=(q, row_peers[i - 1]), device_id_type=MESH,
        )

    mine_a = (slice(None), pl.ds(pl.multiple_of(r * 16, 16), 16), slice(None))
    copies_a = [gather_copy(wall, mine_a, i, a_send, a_recv) for i in range(1, NROW)]
    for i in (4, 3, 5, 2, 6, 1, 7):
        copies_a[i - 1].start()

    for n in (7, 9, 10):
        loads[n].wait()
    spots = place(v_red2[...].astype(F32), 256.0, 96.0)
    valid = jnp.where(v_near2[...] >= 0, 1.0, 0.0)
    valid = (valid[:, 0:1], valid[:, 1:2])
    for d in range(NROW):
        moved = nt(v_w2[0:96, :], one_hot(spots, d * 256, 256, 192))
        for n in range(2):
            part = moved[n * 48 : n * 48 + 48] * valid[n]
            deal_send[d, n * 48 : n * 48 + 48, :] = part[:, 0:128].astype(BF16)
            rest = jnp.where(low, part[0:24, 128:256], part[24:48, 128:256])
            deal_rest[d, n * 24 : n * 24 + 24, :] = rest
        deal_send[d, 96:144, :] = deal_rest[d].astype(BF16)
    deal_recv[r] = deal_send[r]
    copies_w = []
    for i in (4, 3, 5, 2, 6, 1, 7):
        copy = pltpu.make_async_remote_copy(
            src_ref=deal_send.at[row_peers[i - 1]], dst_ref=deal_recv.at[r],
            send_sem=w_send.at[i - 1], recv_sem=w_recv.at[i - 1],
            device_id=(q, row_peers[i - 1]), device_id_type=MESH,
        )
        copy.start()
        copies_w.append(copy)

    loads[3].wait()
    loads[4].wait()
    dof_lane = lax.broadcasted_iota(jnp.int32, (24, 320), 1).astype(F32)
    pick = (
        lax.broadcasted_iota(jnp.int32, (24, 192), 1)
        == lax.broadcasted_iota(jnp.int32, (24, 192), 0) + r * 24
    )
    for b in range(4):
        parts = []
        for h in range(2):
            box = b + 4 * h
            names = v_skel1[box : box + 1, :].astype(F32)
            column = jnp.sum(jnp.where(pick, names, 0.0), axis=1, keepdims=True)
            onehot = jnp.where(dof_lane == column, 1.0, 0.0).astype(BF16)
            parts.append(nt(onehot, rhs16[b]) - nt(v_interp1[box], xr[b]))
        ys[b * 24 : b * 24 + 24, :] = jnp.where(low, parts[0], parts[1])

    loads[5].wait()
    loads[6].wait()
    names = v_near1[...]
    relative = (names - 8 * (q - 2)).astype(F32)
    group = jnp.floor(relative * 0.125)
    child = relative - 8.0 * group
    spot = jnp.where(group == 0.0, 0.0, 4.0)
    for n, step in enumerate(STEPS):
        spot = jnp.where(group == step + 2.0, float(n), spot)
    half = jnp.floor(child * 0.25)
    quarter = child - 4.0 * half
    chunk = jnp.floor(quarter * 0.5)
    relative = 480.0 * chunk + 96.0 * spot + 48.0 * half + 24.0 * (quarter - 2.0 * chunk)
    relative = jnp.where(names < 0, -64.0, relative)
    lane = lax.broadcasted_iota(jnp.int32, (8, 192), 1).astype(F32)
    slot = jnp.floor((lane + 0.5) * (1.0 / 24.0))
    key = lane - 24.0 * slot
    for j in range(8):
        key = key + jnp.where(slot == float(j), relative[:, j : j + 1], 0.0)
    for box in range(8):
        h, b = box // 4, box % 4
        for start in range(0, 960, 240):
            moved = nn(one_hot(key[box : box + 1, :], start, 240), v_couple[box])
            routed[h * 960 + start : h * 960 + start + 240, b * 128 : b * 128 + 128] = moved.astype(BF16)

    for copy in copies_a:
        copy.wait_recv()

    w = wall[...].reshape(512, 128)

    def updates(start, count):
        top = nn(routed[start : start + 96 * count, :], w)
        bottom = nn(routed[960 + start : 960 + start + 96 * count, :], w)
        totals = []
        for n in range(count):
            a = slice(96 * n, 96 * n + 48)
            b = slice(96 * n + 48, 96 * n + 96)
            keep = jnp.where(low, top[a], bottom[b])
            turn = jnp.where(low, top[b], bottom[a])
            totals.append(keep + pltpu.roll(turn, 64, 1))
        return totals

    def box_copy(n, chunk):
        part = pl.ds(chunk * 48, 48)
        return pltpu.make_async_remote_copy(
            src_ref=box_send.at[n, part], dst_ref=box_recv.at[n, part],
            send_sem=b_send.at[chunk, n], recv_sem=b_recv.at[chunk, n],
            device_id=(box_peers[n], r), device_id_type=MESH,
        )

    for n, step in enumerate((-1, 1)):

        @pl.when(inside(q - step, nbox))
        def _():
            pl.semaphore_wait(ready.at[n], 1)

    for chunk in range(2):
        for n, total in enumerate(updates(480 * chunk, 4)):
            box_send[n, chunk * 48 : chunk * 48 + 48, :] = total.astype(BF16)
        for n, step in enumerate(STEPS):

            @pl.when(inside(q + step, nbox))
            def _():
                box_copy(n, chunk).start()

    for chunk in range(2):
        part = slice(chunk * 48, chunk * 48 + 48)
        own[part, :] = updates(480 * chunk + 384, 1)[0] + ys[part, :]

    for n in (8, 11, 12):
        loads[n].wait()
    spots = place(v_red2[...].astype(F32), 96.0, 768.0)
    pick2 = (
        lax.broadcasted_iota(jnp.int32, (48, 384), 1)
        == lax.broadcasted_iota(jnp.int32, (48, 384), 0) + r * 48
    )
    mine = jnp.sum(jnp.where(pick2, place(v_skel2[...].astype(F32), 96.0, 768.0), 0.0), axis=1, keepdims=True)
    spot_lane = lax.broadcasted_iota(jnp.int32, (48, 256), 1)
    mine = mine.astype(jnp.int32)

    def scatter(i):
        h, j = i // 3, i % 3
        moved = nt(v_w2[96:288, :], one_hot(spots, i * 256, 256))
        chosen = jnp.where(spot_lane + i * 256 == mine, 1.0, 0.0)
        lanes = slice(j * 256, j * 256 + 256)
        w2s[h * 192 : h * 192 + 48, lanes] = (chosen - moved[0:48]).astype(BF16)
        w2s[h * 192 + 48 : h * 192 + 192, lanes] = moved[48:192].astype(BF16)

    for i in range(3):
        scatter(i)

    copies_c = []
    for chunk in range(2):
        for n, step in enumerate(STEPS):

            @pl.when(inside(q - step, nbox))
            def _():
                box_copy(n, chunk).wait_recv()

        part = slice(chunk * 48, chunk * 48 + 48)
        z = own[part, :]
        for n in range(4):
            z = z + box_recv[n, part, :].astype(F32)
        rows = pl.ds(pl.multiple_of(r * 96 + chunk * 48, 16), 48)
        own[part, :] = z
        parent[rows, :] = z.astype(BF16)
        for i in (4, 3, 5, 2, 6, 1, 7):
            copies_c.append(gather_copy(parent, (rows, slice(None)), i, c_send.at[chunk], c_recv.at[chunk]))
            copies_c[-1].start()

    for copy in copies_w:
        copy.wait_recv()
    block = own[...]
    turned = pltpu.roll(block, 64, 1)
    lower = jnp.where(low, block, turned)
    upper = jnp.where(low, turned, block)
    first = jnp.concatenate([lower, upper[0:32]], axis=0).astype(BF16)
    tail = upper[32:96]
    second = jnp.concatenate([jnp.where(low, tail, 0.0), jnp.where(low, 0.0, tail)], axis=0).astype(BF16)

    def pair_copy(n, step, row):
        return pltpu.make_async_remote_copy(
            src_ref=pair_send.at[n, row], dst_ref=pair_recv.at[n, r],
            send_sem=d_send.at[n, row], recv_sem=d_recv.at[n, r],
            device_id=(q + step, row), device_id_type=MESH,
        )

    def pair_arrival(n, row):
        return pltpu.make_async_remote_copy(
            src_ref=pair_send.at[n, row], dst_ref=pair_recv.at[n, row],
            send_sem=d_send.at[n, row], recv_sem=d_recv.at[n, row],
            device_id=(q, row), device_id_type=MESH,
        )

    for row in range(NROW):
        main = nn(deal_recv[row, 0:96, :], first)
        rest = nn(deal_recv[row, 96:144, :], second)
        for n in range(2):
            a = n * 48
            total = jnp.where(low, main[a : a + 24], main[a + 24 : a + 48]) + rest[n * 24 : n * 24 + 24]
            pair_send[n, row] = total.astype(BF16)
    for n, step in enumerate((-1, 1)):

        @pl.when(inside(q + step, nbox))
        def _():
            for row in range(NROW):
                pair_copy(n, step, row).start()

    for i in range(3, 6):
        scatter(i)

    for copy in copies_c:
        copy.wait_recv()

    p = parent[...]
    skel = nn(w2s[0:48, :], p) + pltpu.roll(nn(w2s[192:240, :], p), 64, 1)

    def tn(a, b):
        return lax.dot_general(a, b, (((0,), (1,)), ((), ())), preferred_element_type=F32)

    two_buf[...] = tn(p, w2s[48:192, :])[0:64] + tn(p, w2s[240:384, :])[64:128]

    for n, step in enumerate((-1, 1)):

        @pl.when(inside(q - step, nbox))
        def _():
            for row in range(NROW):
                pair_arrival(n, row).wait_recv()

    pairs = jnp.sum(pair_recv[...].astype(F32).reshape(16, 24, 128), axis=0)
    skel_buf[0:24, :] = (skel[0:24] + pairs)[:, 0:64]
    skel_buf[24:48, :] = (skel[24:48] + pltpu.roll(pairs, 64, 1))[:, 0:64]
    for n, step in enumerate(STEPS):

        @pl.when(inside(q + step, nbox))
        def _():
            box_copy(n, 0).wait_send()
            box_copy(n, 1).wait_send()

    for n, step in enumerate((-1, 1)):

        @pl.when(inside(q + step, nbox))
        def _():
            for row in range(NROW):
                pair_copy(n, step, row).wait_send()

    for copy in copies_a + copies_w + copies_c:
        copy.wait_send()


def finish(one, two, skel, out_one, out_two, out_skel, sem):
    copies = [
        pltpu.make_async_copy(source, target, sem.at[n])
        for n, (source, target) in enumerate(((one, out_one), (two, out_two), (skel, out_skel)))
    ]
    for copy in copies:
        copy.start()
    for copy in copies:
        copy.wait()


def shards(nbox, rhs, skel1, red1, interp1, inv1, couple1, near1, skel2, red2, interp2, inv2, panel2, near2):
    turned = lambda a: jnp.swapaxes(a, -1, -2)
    operands = (
        rhs.reshape(512, 320), skel1, red1, turned(interp1), turned(inv1),
        turned(couple1).reshape(8, 192, 128), near1, skel2, red2,
        turned(interp2).reshape(48, 1152), turned(inv2).reshape(144, 1152),
        turned(panel2).reshape(96, 1152), near2,
    )
    dma = pltpu.SemaphoreType.DMA
    one, two, skel = pl.pallas_call(
        functools.partial(kernel, nbox),
        out_shape=tuple(pltpu.VMEM(shape, F32) for shape in SHAPES),
        in_specs=[pl.BlockSpec(memory_space=pl.ANY)] * len(operands),
        out_specs=(pl.BlockSpec(memory_space=pltpu.VMEM),) * 3,
        scratch_shapes=[
            pltpu.VMEM((512, 320), F32),
            pltpu.VMEM((8, 192), jnp.int32),
            pltpu.VMEM((8, 128), jnp.int32),
            pltpu.VMEM((8, 24, 128), BF16),
            pltpu.VMEM((8, 16, 128), BF16),
            pltpu.VMEM((8, 192, 128), BF16),
            pltpu.VMEM((8, 8), jnp.int32),
            pltpu.VMEM((1, 384), jnp.int32),
            pltpu.VMEM((1, 1152), jnp.int32),
            pltpu.VMEM((288, 1152), BF16),
            pltpu.VMEM((1, 2), jnp.int32),
            pltpu.VMEM((4, 128, 320), BF16),
            pltpu.VMEM((4, 128, 128), BF16),
            pltpu.VMEM((4, 128, 128), BF16),
            pltpu.VMEM((1920, 512), BF16),
            pltpu.VMEM((96, 128), F32),
            pltpu.VMEM((96, 128), F32),
            pltpu.VMEM((4, 96, 128), BF16),
            pltpu.VMEM((4, 96, 128), BF16),
            pltpu.VMEM((768, 128), BF16),
            pltpu.VMEM((384, 768), BF16),
            pltpu.VMEM((2, NROW, 24, 128), BF16),
            pltpu.VMEM((2, NROW, 24, 128), BF16),
            dma((13,)),
            dma((7,)), dma((7,)), dma((2, 4)), dma((2, 4)), dma((2, 7)), dma((2, 7)), dma((2, 8)), dma((2, 8)),
            pltpu.VMEM((NROW, 144, 128), BF16),
            pltpu.VMEM((NROW, 144, 128), BF16),
            pltpu.VMEM((NROW, 48, 128), F32),
            dma((7,)), dma((7,)), pltpu.SemaphoreType.REGULAR((2,)),
        ],
        compiler_params=pltpu.CompilerParams(
            collective_id=0, has_side_effects=True, vmem_limit_bytes=60 << 20
        ),
        name="skeleton_step",
    )(*operands)
    one, two, skel = pl.pallas_call(
        finish,
        out_shape=tuple(jax.ShapeDtypeStruct(shape, F32) for shape in SHAPES),
        in_specs=[pl.BlockSpec(memory_space=pltpu.VMEM)] * 3,
        out_specs=(pl.BlockSpec(memory_space=pl.ANY),) * 3,
        scratch_shapes=[dma((3,))],
        name="write_results",
    )(*(pltpu.with_memory_space_constraint(a, pltpu.VMEM) for a in (one, two, skel)))
    return (
        jnp.swapaxes(one.reshape(8, 16, 64), 1, 2),
        two.reshape(1, 64, 144),
        jnp.swapaxes(skel.reshape(1, 48, 64), 1, 2),
    )


def solution(mesh):
    return jax.shard_map(
        functools.partial(shards, mesh.shape["box"]),
        mesh=mesh,
        in_specs=(
            P("box", None, None),
            P("box", None),
            P("box", None),
            P("box", None, "row"),
            P("box", None, "row"),
            P("box", None, None, "row"),
            P("box", None),
            P("box", None),
            P("box", None),
            P("box", None, "row"),
            P("box", None, "row"),
            P("box", None, None, "row"),
            P("box", None),
        ),
        out_specs=(P("box", None, "row"), P("box", None, "row"), P("box", None, "row")),
        check_vma=False,
    )
```

```python
import functools

import jax
import jax.numpy as jnp
from jax import lax
from jax.experimental import pallas as pl
from jax.experimental.pallas import tpu as pltpu
from jax.sharding import PartitionSpec as P

MESH = pl.DeviceIdType.MESH
F32 = jnp.float32
BF16 = jnp.bfloat16
NROW = 8
STEPS = (-2, 2, -1, 1)
SHAPES = ((128, 64), (64, 144), (48, 64))


def nt(a, b):
    return lax.dot_general(a, b, (((1,), (1,)), ((), ())), preferred_element_type=F32)


def nn(a, b):
    return jnp.dot(a, b, preferred_element_type=F32)


def one_hot(targets, start, rows, twice=None):
    shift = targets - float(start)
    shift = jnp.where(shift < float(rows), shift, -1.0).astype(BF16)
    row = lax.broadcasted_iota(jnp.int32, (rows, targets.shape[1]), 0)
    if twice is not None:
        row = jnp.where(row < twice, row, row - (rows - twice))
    row = row.astype(F32).astype(BF16)
    return jnp.where(row == shift, jnp.ones((), BF16), jnp.zeros((), BF16))


def inside(q, nbox):
    return jnp.logical_and(q >= 0, q < nbox)


def place(p, stride, halves):
    box = jnp.floor((p + 0.5) * (1.0 / 192.0))
    rest = p - 192.0 * box
    owner = jnp.floor((rest + 0.5) * (1.0 / 24.0))
    half = jnp.where(box >= 4.0, 1.0, 0.0)
    return stride * owner + halves * half + 24.0 * (box - 4.0 * half) + (rest - 24.0 * owner)


def kernel(
    nbox,
    rhs, skel1, red1, interp1, inv1, couple1, near1, skel2, red2, interp2, inv2, panel2, near2,
    one_buf, two_buf, skel_buf,
    v_rhs, v_skel1, v_red1, v_interp1, v_inv1, v_couple, v_near1, v_skel2, v_red2, v_w2, v_near2,
    rhs16, xr, wall, routed, ys, own, box_send, box_recv, parent, w2s, pair_send, pair_recv,
    load_sem, a_send, a_recv, b_send, b_recv, c_send, c_recv, d_send, d_recv,
    deal_send, deal_recv, deal_rest, w_send, w_recv, ready,
):
    q = lax.axis_index("box")
    r = lax.axis_index("row")

    loads = []
    for source, target in (
        (red1, v_red1), (rhs, v_rhs), (inv1, v_inv1), (skel1, v_skel1), (interp1, v_interp1),
        (near1, v_near1), (couple1, v_couple), (red2, v_red2), (skel2, v_skel2), (near2, v_near2),
        (panel2, v_w2.at[0:96]), (interp2, v_w2.at[96:144]), (inv2, v_w2.at[144:288]),
    ):
        copy = pltpu.make_async_copy(source, target, load_sem.at[len(loads)])
        copy.start()
        loads.append(copy)

    barrier = pltpu.get_barrier_semaphore()
    row_peers = [lax.rem(r + i, NROW) for i in range(1, NROW)]
    box_peers = [q + step for step in STEPS]
    for peer in row_peers:
        pl.semaphore_signal(barrier, inc=1, device_id=(q, peer), device_id_type=MESH)
    for n, step in enumerate((-1, 1)):

        @pl.when(inside(q + step, nbox))
        def _():
            pl.semaphore_signal(barrier, inc=1, device_id=(q + step, r), device_id_type=MESH)

    for n, step in enumerate(STEPS):

        @pl.when(jnp.logical_not(inside(q - step, nbox)))
        def _():
            box_recv[n] = jnp.zeros(box_recv.shape[1:], BF16)

    for n, step in enumerate((-1, 1)):

        @pl.when(jnp.logical_not(inside(q - step, nbox)))
        def _():
            pair_recv[n] = jnp.zeros(pair_recv.shape[1:], BF16)

    low = lax.broadcasted_iota(jnp.int32, (1, 128), 1) < 64

    loads[0].wait()
    loads[1].wait()
    loads[2].wait()
    dof = lax.broadcasted_iota(jnp.int32, (320, 128), 0)
    for b in range(4):
        for h in range(2):
            box = b + 4 * h
            onehot = jnp.where(dof == v_red1[box : box + 1, :], 1.0, 0.0).astype(BF16)
            values = v_rhs[box * 64 : box * 64 + 64, :].astype(BF16)
            rhs16[b, h * 64 : h * 64 + 64, :] = values
            xr[b, h * 64 : h * 64 + 64, :] = nn(values, onehot).astype(BF16)
        x = xr[b]
        first = nt(v_inv1[b], x)
        second = nt(v_inv1[b + 4], x)
        one_buf[b * 16 : b * 16 + 16, :] = first[:, 0:64]
        one_buf[b * 16 + 64 : b * 16 + 80, :] = pltpu.roll(second, 64, 1)[:, 0:64]
        wall[b, pl.ds(pl.multiple_of(r * 16, 16), 16), :] = jnp.where(low, first, second).astype(BF16)

    greeted = sum(inside(q + step, nbox).astype(jnp.int32) for step in (-1, 1))
    pl.semaphore_wait(barrier, NROW - 1 + greeted)

    for n, step in enumerate((-1, 1)):

        @pl.when(inside(q + step, nbox))
        def _():
            pl.semaphore_signal(ready.at[n], inc=1, device_id=(q + step, r), device_id_type=MESH)

    def gather_copy(buffer, index, i, send, recv):
        return pltpu.make_async_remote_copy(
            src_ref=buffer.at[index], dst_ref=buffer.at[index],
            send_sem=send.at[i - 1], recv_sem=recv.at[i - 1],
            device_id=(q, row_peers[i - 1]), device_id_type=MESH,
        )

    mine_a = (slice(None), pl.ds(pl.multiple_of(r * 16, 16), 16), slice(None))
    copies_a = [gather_copy(wall, mine_a, i, a_send, a_recv) for i in range(1, NROW)]
    for i in (4, 3, 5, 2, 6, 1, 7):
        copies_a[i - 1].start()

    loads[3].wait()
    loads[4].wait()
    dof_lane = lax.broadcasted_iota(jnp.int32, (24, 320), 1).astype(F32)
    pick = (
        lax.broadcasted_iota(jnp.int32, (24, 192), 1)
        == lax.broadcasted_iota(jnp.int32, (24, 192), 0) + r * 24
    )
    for b in range(4):
        parts = []
        for h in range(2):
            box = b + 4 * h
            names = v_skel1[box : box + 1, :].astype(F32)
            column = jnp.sum(jnp.where(pick, names, 0.0), axis=1, keepdims=True)
            onehot = jnp.where(dof_lane == column, 1.0, 0.0).astype(BF16)
            parts.append(nt(onehot, rhs16[b]) - nt(v_interp1[box], xr[b]))
        ys[b * 24 : b * 24 + 24, :] = jnp.where(low, parts[0], parts[1])

    for n in (7, 9, 10):
        loads[n].wait()
    spots = place(v_red2[...].astype(F32), 256.0, 96.0)
    valid = jnp.where(v_near2[...] >= 0, 1.0, 0.0)
    valid = (valid[:, 0:1], valid[:, 1:2])
    for d in range(NROW):
        moved = nt(v_w2[0:96, :], one_hot(spots, d * 256, 256, 192))
        for n in range(2):
            part = moved[n * 48 : n * 48 + 48] * valid[n]
            deal_send[d, n * 48 : n * 48 + 48, :] = part[:, 0:128].astype(BF16)
            rest = jnp.where(low, part[0:24, 128:256], part[24:48, 128:256])
            deal_rest[d, n * 24 : n * 24 + 24, :] = rest
        deal_send[d, 96:144, :] = deal_rest[d].astype(BF16)
    deal_recv[r] = deal_send[r]
    copies_w = []
    for i in (4, 3, 5, 2, 6, 1, 7):
        copy = pltpu.make_async_remote_copy(
            src_ref=deal_send.at[row_peers[i - 1]], dst_ref=deal_recv.at[r],
            send_sem=w_send.at[i - 1], recv_sem=w_recv.at[i - 1],
            device_id=(q, row_peers[i - 1]), device_id_type=MESH,
        )
        copy.start()
        copies_w.append(copy)

    loads[5].wait()
    loads[6].wait()
    names = v_near1[...]
    relative = (names - 8 * (q - 2)).astype(F32)
    group = jnp.floor(relative * 0.125)
    child = relative - 8.0 * group
    spot = jnp.where(group == 0.0, 0.0, 4.0)
    for n, step in enumerate(STEPS):
        spot = jnp.where(group == step + 2.0, float(n), spot)
    half = jnp.floor(child * 0.25)
    quarter = child - 4.0 * half
    chunk = jnp.floor(quarter * 0.5)
    ring = jnp.floor(spot * 0.5)
    start = jnp.where(spot == 4.0, 768.0 + 96.0 * chunk, 384.0 * ring + 192.0 * chunk + 96.0 * (spot - 2.0 * ring))
    relative = start + 48.0 * half + 24.0 * (quarter - 2.0 * chunk)
    relative = jnp.where(names < 0, -64.0, relative)
    lane = lax.broadcasted_iota(jnp.int32, (8, 192), 1).astype(F32)
    slot = jnp.floor((lane + 0.5) * (1.0 / 24.0))
    key = lane - 24.0 * slot
    for j in range(8):
        key = key + jnp.where(slot == float(j), relative[:, j : j + 1], 0.0)
    for box in range(8):
        h, b = box // 4, box % 4
        for start in range(0, 960, 240):
            moved = nn(one_hot(key[box : box + 1, :], start, 240), v_couple[box])
            routed[h * 960 + start : h * 960 + start + 240, b * 128 : b * 128 + 128] = moved.astype(BF16)

    for copy in copies_a:
        copy.wait_recv()

    w = wall[...].reshape(512, 128)

    def updates(start, count):
        top = nn(routed[start : start + 96 * count, :], w)
        bottom = nn(routed[960 + start : 960 + start + 96 * count, :], w)
        totals = []
        for n in range(count):
            a = slice(96 * n, 96 * n + 48)
            b = slice(96 * n + 48, 96 * n + 96)
            keep = jnp.where(low, top[a], bottom[b])
            turn = jnp.where(low, top[b], bottom[a])
            totals.append(keep + pltpu.roll(turn, 64, 1))
        return totals

    def box_copy(n, chunk):
        part = pl.ds(chunk * 48, 48)
        return pltpu.make_async_remote_copy(
            src_ref=box_send.at[n, part], dst_ref=box_recv.at[n, part],
            send_sem=b_send.at[chunk, n], recv_sem=b_recv.at[chunk, n],
            device_id=(box_peers[n], r), device_id_type=MESH,
        )

    for n, step in enumerate((-1, 1)):

        @pl.when(inside(q - step, nbox))
        def _():
            pl.semaphore_wait(ready.at[n], 1)

    for ring in range(2):
        for place_in, total in enumerate(updates(384 * ring, 4)):
            chunk, n = place_in // 2, 2 * ring + place_in % 2
            box_send[n, chunk * 48 : chunk * 48 + 48, :] = total.astype(BF16)
        for chunk in range(2):
            for n in (2 * ring, 2 * ring + 1):

                @pl.when(inside(q + STEPS[n], nbox))
                def _():
                    box_copy(n, chunk).start()

    for chunk, total in enumerate(updates(768, 2)):
        part = slice(chunk * 48, chunk * 48 + 48)
        own[part, :] = total + ys[part, :]

    for n in (8, 11, 12):
        loads[n].wait()
    spots = place(v_red2[...].astype(F32), 96.0, 768.0)
    pick2 = (
        lax.broadcasted_iota(jnp.int32, (48, 384), 1)
        == lax.broadcasted_iota(jnp.int32, (48, 384), 0) + r * 48
    )
    mine = jnp.sum(jnp.where(pick2, place(v_skel2[...].astype(F32), 96.0, 768.0), 0.0), axis=1, keepdims=True)
    spot_lane = lax.broadcasted_iota(jnp.int32, (48, 256), 1)
    mine = mine.astype(jnp.int32)

    def scatter(i):
        h, j = i // 3, i % 3
        moved = nt(v_w2[96:288, :], one_hot(spots, i * 256, 256))
        chosen = jnp.where(spot_lane + i * 256 == mine, 1.0, 0.0)
        lanes = slice(j * 256, j * 256 + 256)
        w2s[h * 192 : h * 192 + 48, lanes] = (chosen - moved[0:48]).astype(BF16)
        w2s[h * 192 + 48 : h * 192 + 192, lanes] = moved[48:192].astype(BF16)

    for i in range(3):
        scatter(i)

    copies_c = []
    for chunk in range(2):
        for n, step in enumerate(STEPS):

            @pl.when(inside(q - step, nbox))
            def _():
                box_copy(n, chunk).wait_recv()

        part = slice(chunk * 48, chunk * 48 + 48)
        z = own[part, :]
        for n in range(4):
            z = z + box_recv[n, part, :].astype(F32)
        rows = pl.ds(pl.multiple_of(r * 96 + chunk * 48, 16), 48)
        own[part, :] = z
        parent[rows, :] = z.astype(BF16)
        for i in (4, 3, 5, 2, 6, 1, 7):
            copies_c.append(gather_copy(parent, (rows, slice(None)), i, c_send.at[chunk], c_recv.at[chunk]))
            if chunk == 0:
                copies_c[-1].start()

    for copy in copies_w:
        copy.wait_recv()
    block = own[...]
    turned = pltpu.roll(block, 64, 1)
    lower = jnp.where(low, block, turned)
    upper = jnp.where(low, turned, block)
    first = jnp.concatenate([lower, upper[0:32]], axis=0).astype(BF16)
    tail = upper[32:96]
    second = jnp.concatenate([jnp.where(low, tail, 0.0), jnp.where(low, 0.0, tail)], axis=0).astype(BF16)

    def pair_copy(n, step, row):
        return pltpu.make_async_remote_copy(
            src_ref=pair_send.at[n, row], dst_ref=pair_recv.at[n, r],
            send_sem=d_send.at[n, row], recv_sem=d_recv.at[n, r],
            device_id=(q + step, row), device_id_type=MESH,
        )

    def pair_arrival(n, row):
        return pltpu.make_async_remote_copy(
            src_ref=pair_send.at[n, row], dst_ref=pair_recv.at[n, row],
            send_sem=d_send.at[n, row], recv_sem=d_recv.at[n, row],
            device_id=(q, row), device_id_type=MESH,
        )

    for row in range(NROW):
        main = nn(deal_recv[row, 0:96, :], first)
        rest = nn(deal_recv[row, 96:144, :], second)
        for n in range(2):
            a = n * 48
            total = jnp.where(low, main[a : a + 24], main[a + 24 : a + 48]) + rest[n * 24 : n * 24 + 24]
            pair_send[n, row] = total.astype(BF16)
    for n, step in enumerate((-1, 1)):

        @pl.when(inside(q + step, nbox))
        def _():
            for row in range(NROW):
                pair_copy(n, step, row).start()

    for copy in copies_c[7:]:
        copy.start()

    for i in range(3, 6):
        scatter(i)

    for copy in copies_c:
        copy.wait_recv()

    p = parent[...]
    skel = nn(w2s[0:48, :], p) + pltpu.roll(nn(w2s[192:240, :], p), 64, 1)

    def tn(a, b):
        return lax.dot_general(a, b, (((0,), (1,)), ((), ())), preferred_element_type=F32)

    two_buf[...] = tn(p, w2s[48:192, :])[0:64] + tn(p, w2s[240:384, :])[64:128]

    for n, step in enumerate((-1, 1)):

        @pl.when(inside(q - step, nbox))
        def _():
            for row in range(NROW):
                pair_arrival(n, row).wait_recv()

    pairs = jnp.sum(pair_recv[...].astype(F32).reshape(16, 24, 128), axis=0)
    skel_buf[0:24, :] = (skel[0:24] + pairs)[:, 0:64]
    skel_buf[24:48, :] = (skel[24:48] + pltpu.roll(pairs, 64, 1))[:, 0:64]
    for n, step in enumerate(STEPS):

        @pl.when(inside(q + step, nbox))
        def _():
            box_copy(n, 0).wait_send()
            box_copy(n, 1).wait_send()

    for n, step in enumerate((-1, 1)):

        @pl.when(inside(q + step, nbox))
        def _():
            for row in range(NROW):
                pair_copy(n, step, row).wait_send()

    for copy in copies_a + copies_w + copies_c:
        copy.wait_send()


def finish(one, two, skel, out_one, out_two, out_skel, sem):
    copies = [
        pltpu.make_async_copy(source, target, sem.at[n])
        for n, (source, target) in enumerate(((one, out_one), (two, out_two), (skel, out_skel)))
    ]
    for copy in copies:
        copy.start()
    for copy in copies:
        copy.wait()


def shards(nbox, rhs, skel1, red1, interp1, inv1, couple1, near1, skel2, red2, interp2, inv2, panel2, near2):
    turned = lambda a: jnp.swapaxes(a, -1, -2)
    operands = (
        rhs.reshape(512, 320), skel1, red1, turned(interp1), turned(inv1),
        turned(couple1).reshape(8, 192, 128), near1, skel2, red2,
        turned(interp2).reshape(48, 1152), turned(inv2).reshape(144, 1152),
        turned(panel2).reshape(96, 1152), near2,
    )
    dma = pltpu.SemaphoreType.DMA
    one, two, skel = pl.pallas_call(
        functools.partial(kernel, nbox),
        out_shape=tuple(pltpu.VMEM(shape, F32) for shape in SHAPES),
        in_specs=[pl.BlockSpec(memory_space=pl.ANY)] * len(operands),
        out_specs=(pl.BlockSpec(memory_space=pltpu.VMEM),) * 3,
        scratch_shapes=[
            pltpu.VMEM((512, 320), F32),
            pltpu.VMEM((8, 192), jnp.int32),
            pltpu.VMEM((8, 128), jnp.int32),
            pltpu.VMEM((8, 24, 128), BF16),
            pltpu.VMEM((8, 16, 128), BF16),
            pltpu.VMEM((8, 192, 128), BF16),
            pltpu.VMEM((8, 8), jnp.int32),
            pltpu.VMEM((1, 384), jnp.int32),
            pltpu.VMEM((1, 1152), jnp.int32),
            pltpu.VMEM((288, 1152), BF16),
            pltpu.VMEM((1, 2), jnp.int32),
            pltpu.VMEM((4, 128, 320), BF16),
            pltpu.VMEM((4, 128, 128), BF16),
            pltpu.VMEM((4, 128, 128), BF16),
            pltpu.VMEM((1920, 512), BF16),
            pltpu.VMEM((96, 128), F32),
            pltpu.VMEM((96, 128), F32),
            pltpu.VMEM((4, 96, 128), BF16),
            pltpu.VMEM((4, 96, 128), BF16),
            pltpu.VMEM((768, 128), BF16),
            pltpu.VMEM((384, 768), BF16),
            pltpu.VMEM((2, NROW, 24, 128), BF16),
            pltpu.VMEM((2, NROW, 24, 128), BF16),
            dma((13,)),
            dma((7,)), dma((7,)), dma((2, 4)), dma((2, 4)), dma((2, 7)), dma((2, 7)), dma((2, 8)), dma((2, 8)),
            pltpu.VMEM((NROW, 144, 128), BF16),
            pltpu.VMEM((NROW, 144, 128), BF16),
            pltpu.VMEM((NROW, 48, 128), F32),
            dma((7,)), dma((7,)), pltpu.SemaphoreType.REGULAR((2,)),
        ],
        compiler_params=pltpu.CompilerParams(
            collective_id=0, has_side_effects=True, vmem_limit_bytes=60 << 20
        ),
        name="skeleton_step",
    )(*operands)
    one, two, skel = pl.pallas_call(
        finish,
        out_shape=tuple(jax.ShapeDtypeStruct(shape, F32) for shape in SHAPES),
        in_specs=[pl.BlockSpec(memory_space=pltpu.VMEM)] * 3,
        out_specs=(pl.BlockSpec(memory_space=pl.ANY),) * 3,
        scratch_shapes=[dma((3,))],
        name="write_results",
    )(*(pltpu.with_memory_space_constraint(a, pltpu.VMEM) for a in (one, two, skel)))
    return (
        jnp.swapaxes(one.reshape(8, 16, 64), 1, 2),
        two.reshape(1, 64, 144),
        jnp.swapaxes(skel.reshape(1, 48, 64), 1, 2),
    )


def solution(mesh):
    return jax.shard_map(
        functools.partial(shards, mesh.shape["box"]),
        mesh=mesh,
        in_specs=(
            P("box", None, None),
            P("box", None),
            P("box", None),
            P("box", None, "row"),
            P("box", None, "row"),
            P("box", None, None, "row"),
            P("box", None),
            P("box", None),
            P("box", None),
            P("box", None, "row"),
            P("box", None, "row"),
            P("box", None, None, "row"),
            P("box", None),
        ),
        out_specs=(P("box", None, "row"), P("box", None, "row"), P("box", None, "row")),
        check_vma=False,
    )
```

```python
import functools

import jax
import jax.numpy as jnp
from jax import lax
from jax.experimental import pallas as pl
from jax.experimental.pallas import tpu as pltpu
from jax.sharding import PartitionSpec as P

MESH = pl.DeviceIdType.MESH
F32 = jnp.float32
BF16 = jnp.bfloat16
NROW = 8
STEPS = (-2, 2, -1, 1)
SHAPES = ((128, 64), (64, 144), (48, 64))


def nt(a, b):
    return lax.dot_general(a, b, (((1,), (1,)), ((), ())), preferred_element_type=F32)


def nn(a, b):
    return jnp.dot(a, b, preferred_element_type=F32)


def one_hot(targets, start, rows, twice=None):
    shift = targets - float(start)
    shift = jnp.where(shift < float(rows), shift, -1.0).astype(BF16)
    row = lax.broadcasted_iota(jnp.int32, (rows, targets.shape[1]), 0)
    if twice is not None:
        row = jnp.where(row < twice, row, row - (rows - twice))
    row = row.astype(F32).astype(BF16)
    return jnp.where(row == shift, jnp.ones((), BF16), jnp.zeros((), BF16))


def inside(q, nbox):
    return jnp.logical_and(q >= 0, q < nbox)


def place(p, stride, halves):
    box = jnp.floor((p + 0.5) * (1.0 / 192.0))
    rest = p - 192.0 * box
    owner = jnp.floor((rest + 0.5) * (1.0 / 24.0))
    half = jnp.where(box >= 4.0, 1.0, 0.0)
    return stride * owner + halves * half + 24.0 * (box - 4.0 * half) + (rest - 24.0 * owner)


def kernel(
    nbox,
    rhs, skel1, red1, interp1, inv1, couple1, near1, skel2, red2, interp2, inv2, panel2, near2,
    one_buf, two_buf, skel_buf,
    v_rhs, v_skel1, v_red1, v_interp1, v_inv1, v_couple, v_near1, v_skel2, v_red2, v_w2, v_near2,
    rhs16, xr, wall, routed, ys, own, box_send, box_recv, parent, w2s, pair_send, pair_recv,
    load_sem, a_send, a_recv, b_send, b_recv, c_send, c_recv, d_send, d_recv,
    deal_send, deal_recv, deal_rest, w_send, w_recv, ready,
):
    q = lax.axis_index("box")
    r = lax.axis_index("row")

    barrier = pltpu.get_barrier_semaphore()
    row_peers = [lax.rem(r + i, NROW) for i in range(1, NROW)]
    box_peers = [q + step for step in STEPS]
    for i in (4, 3, 5, 2, 6, 1, 7):
        pl.semaphore_signal(barrier, inc=1, device_id=(q, row_peers[i - 1]), device_id_type=MESH)
    for n, step in enumerate((-1, 1)):

        @pl.when(inside(q + step, nbox))
        def _():
            pl.semaphore_signal(barrier, inc=1, device_id=(q + step, r), device_id_type=MESH)

    loads = []
    for source, target in (
        (red1, v_red1), (rhs, v_rhs), (inv1, v_inv1), (skel1, v_skel1), (interp1, v_interp1),
        (near1, v_near1), (couple1, v_couple), (red2, v_red2), (skel2, v_skel2), (near2, v_near2),
        (panel2, v_w2.at[0:96]), (interp2, v_w2.at[96:144]), (inv2, v_w2.at[144:288]),
    ):
        copy = pltpu.make_async_copy(source, target, load_sem.at[len(loads)])
        copy.start()
        loads.append(copy)

    for n, step in enumerate(STEPS):

        @pl.when(jnp.logical_not(inside(q - step, nbox)))
        def _():
            box_recv[n] = jnp.zeros(box_recv.shape[1:], BF16)

    for n, step in enumerate((-1, 1)):

        @pl.when(jnp.logical_not(inside(q - step, nbox)))
        def _():
            pair_recv[n] = jnp.zeros(pair_recv.shape[1:], BF16)

    low = lax.broadcasted_iota(jnp.int32, (1, 128), 1) < 64

    loads[0].wait()
    loads[1].wait()
    loads[2].wait()
    dof = lax.broadcasted_iota(jnp.int32, (320, 128), 0)
    for b in range(4):
        for h in range(2):
            box = b + 4 * h
            onehot = jnp.where(dof == v_red1[box : box + 1, :], 1.0, 0.0).astype(BF16)
            values = v_rhs[box * 64 : box * 64 + 64, :].astype(BF16)
            rhs16[b, h * 64 : h * 64 + 64, :] = values
            xr[b, h * 64 : h * 64 + 64, :] = nn(values, onehot).astype(BF16)
        x = xr[b]
        first = nt(v_inv1[b], x)
        second = nt(v_inv1[b + 4], x)
        one_buf[b * 16 : b * 16 + 16, :] = first[:, 0:64]
        one_buf[b * 16 + 64 : b * 16 + 80, :] = pltpu.roll(second, 64, 1)[:, 0:64]
        wall[b, pl.ds(pl.multiple_of(r * 16, 16), 16), :] = jnp.where(low, first, second).astype(BF16)

    greeted = sum(inside(q + step, nbox).astype(jnp.int32) for step in (-1, 1))
    pl.semaphore_wait(barrier, NROW - 1 + greeted)

    for n, step in enumerate((-1, 1)):

        @pl.when(inside(q + step, nbox))
        def _():
            pl.semaphore_signal(ready.at[n], inc=1, device_id=(q + step, r), device_id_type=MESH)

    def gather_copy(buffer, index, i, send, recv):
        return pltpu.make_async_remote_copy(
            src_ref=buffer.at[index], dst_ref=buffer.at[index],
            send_sem=send.at[i - 1], recv_sem=recv.at[i - 1],
            device_id=(q, row_peers[i - 1]), device_id_type=MESH,
        )

    mine_a = (slice(None), pl.ds(pl.multiple_of(r * 16, 16), 16), slice(None))
    copies_a = [gather_copy(wall, mine_a, i, a_send, a_recv) for i in range(1, NROW)]
    for i in (4, 3, 5, 2, 6, 1, 7):
        copies_a[i - 1].start()

    loads[3].wait()
    loads[4].wait()
    dof_lane = lax.broadcasted_iota(jnp.int32, (24, 320), 1).astype(F32)
    pick = (
        lax.broadcasted_iota(jnp.int32, (24, 192), 1)
        == lax.broadcasted_iota(jnp.int32, (24, 192), 0) + r * 24
    )
    for b in range(4):
        parts = []
        for h in range(2):
            box = b + 4 * h
            names = v_skel1[box : box + 1, :].astype(F32)
            column = jnp.sum(jnp.where(pick, names, 0.0), axis=1, keepdims=True)
            onehot = jnp.where(dof_lane == column, 1.0, 0.0).astype(BF16)
            parts.append(nt(onehot, rhs16[b]) - nt(v_interp1[box], xr[b]))
        ys[b * 24 : b * 24 + 24, :] = jnp.where(low, parts[0], parts[1])

    for n in (7, 9, 10):
        loads[n].wait()
    spots = place(v_red2[...].astype(F32), 256.0, 96.0)
    valid = jnp.where(v_near2[...] >= 0, 1.0, 0.0)
    valid = (valid[:, 0:1], valid[:, 1:2])
    for d in range(NROW):
        moved = nt(v_w2[0:96, :], one_hot(spots, d * 256, 256, 192))
        for n in range(2):
            part = moved[n * 48 : n * 48 + 48] * valid[n]
            deal_send[d, n * 48 : n * 48 + 48, :] = part[:, 0:128].astype(BF16)
            rest = jnp.where(low, part[0:24, 128:256], part[24:48, 128:256])
            deal_rest[d, n * 24 : n * 24 + 24, :] = rest
        deal_send[d, 96:144, :] = deal_rest[d].astype(BF16)
    deal_recv[r] = deal_send[r]
    copies_w = []
    for i in (4, 3, 5, 2, 6, 1, 7):
        copy = pltpu.make_async_remote_copy(
            src_ref=deal_send.at[row_peers[i - 1]], dst_ref=deal_recv.at[r],
            send_sem=w_send.at[i - 1], recv_sem=w_recv.at[i - 1],
            device_id=(q, row_peers[i - 1]), device_id_type=MESH,
        )
        copy.start()
        copies_w.append(copy)

    loads[5].wait()
    loads[6].wait()
    names = v_near1[...]
    relative = (names - 8 * (q - 2)).astype(F32)
    group = jnp.floor(relative * 0.125)
    child = relative - 8.0 * group
    spot = jnp.where(group == 0.0, 0.0, 4.0)
    for n, step in enumerate(STEPS):
        spot = jnp.where(group == step + 2.0, float(n), spot)
    half = jnp.floor(child * 0.25)
    quarter = child - 4.0 * half
    chunk = jnp.floor(quarter * 0.5)
    ring = jnp.floor(spot * 0.5)
    start = jnp.where(spot == 4.0, 768.0 + 96.0 * chunk, 384.0 * ring + 192.0 * chunk + 96.0 * (spot - 2.0 * ring))
    relative = start + 48.0 * half + 24.0 * (quarter - 2.0 * chunk)
    relative = jnp.where(names < 0, -64.0, relative)
    lane = lax.broadcasted_iota(jnp.int32, (8, 192), 1).astype(F32)
    slot = jnp.floor((lane + 0.5) * (1.0 / 24.0))
    key = lane - 24.0 * slot
    for j in range(8):
        key = key + jnp.where(slot == float(j), relative[:, j : j + 1], 0.0)
    for box in range(8):
        h, b = box // 4, box % 4
        for start in range(0, 960, 240):
            moved = nn(one_hot(key[box : box + 1, :], start, 240), v_couple[box])
            routed[h * 960 + start : h * 960 + start + 240, b * 128 : b * 128 + 128] = moved.astype(BF16)

    for copy in copies_a:
        copy.wait_recv()

    w = wall[...].reshape(512, 128)

    def updates(start, count):
        top = nn(routed[start : start + 96 * count, :], w)
        bottom = nn(routed[960 + start : 960 + start + 96 * count, :], w)
        totals = []
        for n in range(count):
            a = slice(96 * n, 96 * n + 48)
            b = slice(96 * n + 48, 96 * n + 96)
            keep = jnp.where(low, top[a], bottom[b])
            turn = jnp.where(low, top[b], bottom[a])
            totals.append(keep + pltpu.roll(turn, 64, 1))
        return totals

    def box_copy(n, chunk):
        part = pl.ds(chunk * 48, 48)
        return pltpu.make_async_remote_copy(
            src_ref=box_send.at[n, part], dst_ref=box_recv.at[n, part],
            send_sem=b_send.at[chunk, n], recv_sem=b_recv.at[chunk, n],
            device_id=(box_peers[n], r), device_id_type=MESH,
        )

    for n, step in enumerate((-1, 1)):

        @pl.when(inside(q - step, nbox))
        def _():
            pl.semaphore_wait(ready.at[n], 1)

    for ring in range(2):
        for place_in, total in enumerate(updates(384 * ring, 4)):
            chunk, n = place_in // 2, 2 * ring + place_in % 2
            box_send[n, chunk * 48 : chunk * 48 + 48, :] = total.astype(BF16)
        for chunk in range(2):
            for n in (2 * ring, 2 * ring + 1):

                @pl.when(inside(q + STEPS[n], nbox))
                def _():
                    box_copy(n, chunk).start()

    for chunk, total in enumerate(updates(768, 2)):
        part = slice(chunk * 48, chunk * 48 + 48)
        own[part, :] = total + ys[part, :]

    for n in (8, 11, 12):
        loads[n].wait()
    spots = place(v_red2[...].astype(F32), 96.0, 768.0)
    pick2 = (
        lax.broadcasted_iota(jnp.int32, (48, 384), 1)
        == lax.broadcasted_iota(jnp.int32, (48, 384), 0) + r * 48
    )
    mine = jnp.sum(jnp.where(pick2, place(v_skel2[...].astype(F32), 96.0, 768.0), 0.0), axis=1, keepdims=True)
    spot_lane = lax.broadcasted_iota(jnp.int32, (48, 256), 1)
    mine = mine.astype(jnp.int32)

    def scatter(i):
        h, j = i // 3, i % 3
        moved = nt(v_w2[96:288, :], one_hot(spots, i * 256, 256))
        chosen = jnp.where(spot_lane + i * 256 == mine, 1.0, 0.0)
        lanes = slice(j * 256, j * 256 + 256)
        w2s[h * 192 : h * 192 + 48, lanes] = (chosen - moved[0:48]).astype(BF16)
        w2s[h * 192 + 48 : h * 192 + 192, lanes] = moved[48:192].astype(BF16)

    for i in range(3):
        scatter(i)

    copies_c = []
    for chunk in range(2):
        for n, step in enumerate(STEPS):

            @pl.when(inside(q - step, nbox))
            def _():
                box_copy(n, chunk).wait_recv()

        part = slice(chunk * 48, chunk * 48 + 48)
        z = own[part, :]
        for n in range(4):
            z = z + box_recv[n, part, :].astype(F32)
        rows = pl.ds(pl.multiple_of(r * 96 + chunk * 48, 16), 48)
        own[part, :] = z
        parent[rows, :] = z.astype(BF16)
        for i in (4, 3, 5, 2, 6, 1, 7):
            copies_c.append(gather_copy(parent, (rows, slice(None)), i, c_send.at[chunk], c_recv.at[chunk]))
            if chunk == 0:
                copies_c[-1].start()

    for copy in copies_w:
        copy.wait_recv()
    block = own[...]
    turned = pltpu.roll(block, 64, 1)
    lower = jnp.where(low, block, turned)
    upper = jnp.where(low, turned, block)
    first = jnp.concatenate([lower, upper[0:32]], axis=0).astype(BF16)
    tail = upper[32:96]
    second = jnp.concatenate([jnp.where(low, tail, 0.0), jnp.where(low, 0.0, tail)], axis=0).astype(BF16)

    def pair_copy(n, step, row):
        return pltpu.make_async_remote_copy(
            src_ref=pair_send.at[n, row], dst_ref=pair_recv.at[n, r],
            send_sem=d_send.at[n, row], recv_sem=d_recv.at[n, r],
            device_id=(q + step, row), device_id_type=MESH,
        )

    def pair_arrival(n, row):
        return pltpu.make_async_remote_copy(
            src_ref=pair_send.at[n, row], dst_ref=pair_recv.at[n, row],
            send_sem=d_send.at[n, row], recv_sem=d_recv.at[n, row],
            device_id=(q, row), device_id_type=MESH,
        )

    for row in range(NROW):
        main = nn(deal_recv[row, 0:96, :], first)
        rest = nn(deal_recv[row, 96:144, :], second)
        for n in range(2):
            a = n * 48
            total = jnp.where(low, main[a : a + 24], main[a + 24 : a + 48]) + rest[n * 24 : n * 24 + 24]
            pair_send[n, row] = total.astype(BF16)
    for n, step in enumerate((-1, 1)):

        @pl.when(inside(q + step, nbox))
        def _():
            for row in range(NROW):
                pair_copy(n, step, row).start()

    for copy in copies_c[7:]:
        copy.start()

    for i in range(3, 6):
        scatter(i)

    for copy in copies_c:
        copy.wait_recv()

    p = parent[...]
    skel = nn(w2s[0:48, :], p) + pltpu.roll(nn(w2s[192:240, :], p), 64, 1)

    def tn(a, b):
        return lax.dot_general(a, b, (((0,), (1,)), ((), ())), preferred_element_type=F32)

    two_buf[...] = tn(p, w2s[48:192, :])[0:64] + tn(p, w2s[240:384, :])[64:128]

    for n, step in enumerate((-1, 1)):

        @pl.when(inside(q - step, nbox))
        def _():
            for row in range(NROW):
                pair_arrival(n, row).wait_recv()

    pairs = jnp.sum(pair_recv[...].astype(F32).reshape(16, 24, 128), axis=0)
    skel_buf[0:24, :] = (skel[0:24] + pairs)[:, 0:64]
    skel_buf[24:48, :] = (skel[24:48] + pltpu.roll(pairs, 64, 1))[:, 0:64]
    for n, step in enumerate(STEPS):

        @pl.when(inside(q + step, nbox))
        def _():
            box_copy(n, 0).wait_send()
            box_copy(n, 1).wait_send()

    for n, step in enumerate((-1, 1)):

        @pl.when(inside(q + step, nbox))
        def _():
            for row in range(NROW):
                pair_copy(n, step, row).wait_send()

    for copy in copies_a + copies_w + copies_c:
        copy.wait_send()


def finish(one, two, skel, out_one, out_two, out_skel, sem):
    copies = [
        pltpu.make_async_copy(source, target, sem.at[n])
        for n, (source, target) in enumerate(((one, out_one), (two, out_two), (skel, out_skel)))
    ]
    for copy in copies:
        copy.start()
    for copy in copies:
        copy.wait()


def shards(nbox, rhs, skel1, red1, interp1, inv1, couple1, near1, skel2, red2, interp2, inv2, panel2, near2):
    turned = lambda a: jnp.swapaxes(a, -1, -2)
    operands = (
        rhs.reshape(512, 320), skel1, red1, turned(interp1), turned(inv1),
        turned(couple1).reshape(8, 192, 128), near1, skel2, red2,
        turned(interp2).reshape(48, 1152), turned(inv2).reshape(144, 1152),
        turned(panel2).reshape(96, 1152), near2,
    )
    dma = pltpu.SemaphoreType.DMA
    one, two, skel = pl.pallas_call(
        functools.partial(kernel, nbox),
        out_shape=tuple(pltpu.VMEM(shape, F32) for shape in SHAPES),
        in_specs=[pl.BlockSpec(memory_space=pl.ANY)] * len(operands),
        out_specs=(pl.BlockSpec(memory_space=pltpu.VMEM),) * 3,
        scratch_shapes=[
            pltpu.VMEM((512, 320), F32),
            pltpu.VMEM((8, 192), jnp.int32),
            pltpu.VMEM((8, 128), jnp.int32),
            pltpu.VMEM((8, 24, 128), BF16),
            pltpu.VMEM((8, 16, 128), BF16),
            pltpu.VMEM((8, 192, 128), BF16),
            pltpu.VMEM((8, 8), jnp.int32),
            pltpu.VMEM((1, 384), jnp.int32),
            pltpu.VMEM((1, 1152), jnp.int32),
            pltpu.VMEM((288, 1152), BF16),
            pltpu.VMEM((1, 2), jnp.int32),
            pltpu.VMEM((4, 128, 320), BF16),
            pltpu.VMEM((4, 128, 128), BF16),
            pltpu.VMEM((4, 128, 128), BF16),
            pltpu.VMEM((1920, 512), BF16),
            pltpu.VMEM((96, 128), F32),
            pltpu.VMEM((96, 128), F32),
            pltpu.VMEM((4, 96, 128), BF16),
            pltpu.VMEM((4, 96, 128), BF16),
            pltpu.VMEM((768, 128), BF16),
            pltpu.VMEM((384, 768), BF16),
            pltpu.VMEM((2, NROW, 24, 128), BF16),
            pltpu.VMEM((2, NROW, 24, 128), BF16),
            dma((13,)),
            dma((7,)), dma((7,)), dma((2, 4)), dma((2, 4)), dma((2, 7)), dma((2, 7)), dma((2, 8)), dma((2, 8)),
            pltpu.VMEM((NROW, 144, 128), BF16),
            pltpu.VMEM((NROW, 144, 128), BF16),
            pltpu.VMEM((NROW, 48, 128), F32),
            dma((7,)), dma((7,)), pltpu.SemaphoreType.REGULAR((2,)),
        ],
        compiler_params=pltpu.CompilerParams(
            collective_id=0, has_side_effects=True, vmem_limit_bytes=60 << 20
        ),
        name="skeleton_step",
    )(*operands)
    one, two, skel = pl.pallas_call(
        finish,
        out_shape=tuple(jax.ShapeDtypeStruct(shape, F32) for shape in SHAPES),
        in_specs=[pl.BlockSpec(memory_space=pltpu.VMEM)] * 3,
        out_specs=(pl.BlockSpec(memory_space=pl.ANY),) * 3,
        scratch_shapes=[dma((3,))],
        name="write_results",
    )(*(pltpu.with_memory_space_constraint(a, pltpu.VMEM) for a in (one, two, skel)))
    return (
        jnp.swapaxes(one.reshape(8, 16, 64), 1, 2),
        two.reshape(1, 64, 144),
        jnp.swapaxes(skel.reshape(1, 48, 64), 1, 2),
    )


def solution(mesh):
    return jax.shard_map(
        functools.partial(shards, mesh.shape["box"]),
        mesh=mesh,
        in_specs=(
            P("box", None, None),
            P("box", None),
            P("box", None),
            P("box", None, "row"),
            P("box", None, "row"),
            P("box", None, None, "row"),
            P("box", None),
            P("box", None),
            P("box", None),
            P("box", None, "row"),
            P("box", None, "row"),
            P("box", None, None, "row"),
            P("box", None),
        ),
        out_specs=(P("box", None, "row"), P("box", None, "row"), P("box", None, "row")),
        check_vma=False,
    )
```
